256 devices in a mesh: leaf: 64 (over z, x, core), sub: 4 (over y).
Axes of the slice: x: 4, y: 4, z: 8, core: 2. Of those that a mesh axis runs over, the one named last changes fastest.
Arguments:
- points: bfloat16 [1048576, 64], P(('leaf', 'sub')), may hold values from -6 to 6
- probes: bfloat16 [1048576, 128], P(('leaf', 'sub')), may hold values from -6 to 6
- order: int32 [1048576], P(('leaf', 'sub')), may hold values from 0 to 511, as said below
- near_lists: int32 [2048, 12], P(('leaf', 'sub')), may hold values from 0 to 2047, as said below
- near_counts: int32 [2048], P(('leaf', 'sub')), may hold values from 1 to 12, as said below
- leaf_sets: int32 [2048, 128], P(('leaf', 'sub')), may hold values from 0 to 511, as said below
- merge_sets: int32 [2047, 128], replicated, may hold values from 0 to 255, as said below
Outputs:
- near_samples: float32 [1048576, 128], P(('leaf', 'sub'))
- root_samples: float32 [16384], P(('leaf', 'sub'))
The draws below stay inside these ranges and needn't reach their ends.
Inputs may be any that keep to these rules, and one draw needn't show every extreme that they name: `order`: the 512 entries of each leaf block are a permutation of 0 to 511. `near_lists`: for block g of shard i = g // 32: entry 0 is g; entries 1 to near_counts[g] - 1 are distinct blocks other than g within i * 32 - 8 to (i + 1) * 32 + 7; entries from near_counts[g] on equal g. `near_counts`: some block among the first sixteen of the aligned sixteens of blocks has 12 entries. `leaf_sets`: each row holds distinct values. `merge_sets`: each row holds distinct values; row m - 1 belongs to the node whose two children meet at block m.
All inputs are finite; a program needn't handle non-finite values.
Results may differ from the reference program's by a relative error of at most 0.0029.
Values may be sent and summed in bfloat16 or wider, within the bound.
A program may use at most 128 MiB of HBM per device.

```python
import jax
import jax.numpy as jnp
from jax import lax

DIM = 64
LEAF = 512
SKEL = 128
PROBES = 128
NEAR = 12
BLK_DEV = 8
SHARD_BLOCKS = 32
NBLOCKS = 2048
NPTS = 1048576


def near_table(key):
    base_key = jax.random.fold_in(key, 71)
    window = SHARD_BLOCKS + 2 * BLK_DEV
    offsets = jnp.arange(window, dtype=jnp.int32)
    slot_ids = jnp.arange(NEAR, dtype=jnp.int32)

    def one_block(block_id):
        block_key = jax.random.fold_in(base_key, block_id)
        shard_id = block_id // SHARD_BLOCKS
        candidate = shard_id * SHARD_BLOCKS - BLK_DEV + offsets
        usable = (candidate >= 0) & (candidate < NBLOCKS) & (candidate != block_id)
        scores = jax.random.permutation(jax.random.fold_in(block_key, 1), window).astype(jnp.int32)
        scores = scores + jnp.where(usable, 0, window)
        ranked = jnp.take(candidate, jnp.argsort(scores), axis=0)[:NEAR - 1]
        first_draw = jax.random.randint(jax.random.fold_in(block_key, 2), (), 1, NEAR + 1)
        second = jax.random.randint(jax.random.fold_in(block_key, 3), (), 1, NEAR + 1)
        live_count = jnp.where(block_id % 16 == 5, NEAR, jnp.minimum(first_draw, second)).astype(jnp.int32)
        listed = jnp.concatenate([block_id[None], ranked])
        listed = jnp.where(slot_ids < live_count, listed, block_id)
        return (listed.astype(jnp.int32), live_count)
    return jax.vmap(one_block)(jnp.arange(NBLOCKS, dtype=jnp.int32))


def draw_near_lists(key, part):
    return near_table(key)[0]


def draw_near_counts(key, part):
    return near_table(key)[1]


def draw_order(key, part):
    base_key = jax.random.fold_in(key, 13)

    def one_block(block_id):
        return jax.random.permutation(jax.random.fold_in(base_key, block_id), LEAF).astype(jnp.int32)
    return jax.vmap(one_block)(jnp.arange(NBLOCKS, dtype=jnp.int32)).reshape(NPTS)


def draw_leaf_sets(key, part):
    base_key = jax.random.fold_in(key, 29)

    def one_block(block_id):
        return jax.random.permutation(jax.random.fold_in(base_key, block_id), LEAF).astype(jnp.int32)[:SKEL]
    return jax.vmap(one_block)(jnp.arange(NBLOCKS, dtype=jnp.int32))


def draw_merge_sets(key, part):
    base_key = jax.random.fold_in(key, 43)

    def one_node(node_id):
        return jax.random.permutation(jax.random.fold_in(base_key, node_id), 2 * SKEL).astype(jnp.int32)[:SKEL]
    return jax.vmap(one_node)(jnp.arange(NBLOCKS - 1, dtype=jnp.int32))


def levels(key, shape, split, least, largest):
    def one(position, blocks):
        draws = jax.random.uniform(jax.random.fold_in(jax.random.fold_in(key, 6), position), (blocks,), jnp.float32, least / len(split), largest / len(split))
        return jnp.repeat(jnp.exp(draws), shape[position] // blocks).reshape((-1,) + (1,) * (len(shape) - position - 1))

    factor_of = one(*split[0])
    for cut in split[1:]:
        factor_of = factor_of * one(*cut)
    return factor_of


def centred(own_key, dims, width, reach, split=(), held_as=jnp.bfloat16):
    gain = levels(own_key, dims, split, -0.22, 0.18) if split else 1.0
    drawn = jax.random.normal(own_key, dims, jnp.float32) * width * gain
    return jnp.minimum(jnp.maximum(drawn, -reach), reach).astype(held_as)


def setup_inputs(seed: int = 0) -> dict:
    key_of = jax.random.split(jax.random.key(seed), 8)
    points = centred(key_of[0], (NPTS, DIM), 1.0, 6.0, ((0, 256),))
    probes = centred(key_of[1], (NPTS, PROBES), 1.0, 6.0, ((0, 256),))
    order = draw_order(jax.random.fold_in(key_of[7], 71), 0)
    near_lists = draw_near_lists(jax.random.fold_in(key_of[7], 71), 0)
    near_counts = draw_near_counts(jax.random.fold_in(key_of[7], 71), 0)
    leaf_sets = draw_leaf_sets(jax.random.fold_in(key_of[7], 71), 0)
    merge_sets = draw_merge_sets(jax.random.fold_in(key_of[7], 71), 0)
    return {"points": points, "probes": probes, "order": order, "near_lists": near_lists, "near_counts": near_counts, "leaf_sets": leaf_sets, "merge_sets": merge_sets}


def row_squares(values):
    return jnp.sum(jnp.square(values.astype(jnp.float32)), axis=-1)


def kernel_tile(target_rows, target_sq, source_rows, source_sq):
    cross_terms = jnp.dot(target_rows, source_rows.T, preferred_element_type=jnp.float32)
    distance = target_sq[:, None] + source_sq[None, :] - 2.0 * cross_terms
    return jnp.exp(-distance / target_rows.shape[1])


def condense(coords, samples, chosen):
    picked = jnp.take(coords, chosen, axis=0)
    weights = kernel_tile(picked, row_squares(picked), coords, row_squares(coords))
    totals = jnp.sum(weights, axis=1, keepdims=True)
    mixed_part = jnp.dot(weights, samples, precision=lax.Precision.HIGHEST, preferred_element_type=jnp.float32)
    return picked, jnp.take(samples, chosen, axis=0) + mixed_part / totals


def reference(points, probes, order, near_lists, near_counts, leaf_sets, merge_sets):
    block_base = (jnp.arange(NPTS).astype(jnp.int32) // LEAF) * LEAF
    tree_points = jnp.take(points, order.astype(jnp.int32) + block_base, axis=0)
    blocks = tree_points.reshape(NBLOCKS, LEAF, DIM)
    probe_blocks = probes.reshape(NBLOCKS, LEAF, PROBES)
    squares = row_squares(blocks)

    def near_block(block_id):
        def add_slot(slot_index, running):
            source = near_lists[block_id, slot_index]
            weights = kernel_tile(blocks[block_id], squares[block_id], blocks[source], squares[source])
            weights = weights.astype(jnp.bfloat16)
            return running + jnp.dot(weights, probe_blocks[source], preferred_element_type=jnp.float32)

        running = lax.fori_loop(0, near_counts[block_id], add_slot, jnp.zeros((LEAF, PROBES), jnp.float32))
        return running * (LEAF ** -0.5)

    near_samples = lax.map(near_block, jnp.arange(NBLOCKS).astype(jnp.int32)).reshape(NPTS, PROBES)

    coords, samples = jax.vmap(condense)(blocks, probe_blocks.astype(jnp.float32), leaf_sets)
    node_span = 1
    while coords.shape[0] > 1:
        node_count = coords.shape[0] // 2
        node_first = jnp.arange(node_count).astype(jnp.int32) * (2 * node_span)
        chosen = jnp.take(merge_sets, node_first + node_span - 1, axis=0)
        coords, samples = jax.vmap(condense)(
            coords.reshape(node_count, 2 * SKEL, DIM),
            samples.reshape(node_count, 2 * SKEL, PROBES),
            chosen)
        node_span = node_span * 2
    return near_samples, samples[0].reshape(SKEL * PROBES)
```

```python
import functools

import jax
import jax.numpy as jnp
from jax import lax
from jax.experimental import pallas as pl
from jax.experimental.pallas import tpu as pltpu
from jax.sharding import PartitionSpec as P

MESH = pl.DeviceIdType.MESH
BF16 = jnp.bfloat16
F32 = jnp.float32
LANES = 128
LEAF = 512
DIM = 64
BLK = 8
HALF = 4
SKEL = 128
RING = 8
LOG2E = 1.4426950408889634
SCALE = 2.0 * LOG2E / DIM


def dot(a, b):
    return jnp.dot(a, b, preferred_element_type=F32)


def dot_nt(a, b):
    return lax.dot_general(a, b, (((1,), (1,)), ((), ())), preferred_element_type=F32)


def split3(h):
    h1 = h.astype(BF16).astype(F32)
    h2 = (h - h1).astype(BF16).astype(F32)
    h3 = (h - h1 - h2).astype(BF16).astype(F32)
    return h1, h2, h3


def one_hot(row, width):
    col = jnp.transpose(jnp.broadcast_to(row, (LANES, LANES)))
    lane = lax.broadcasted_iota(jnp.int32, (LANES, LANES), 1)
    parts = [
        jnp.where(col == lane + j * LANES, 1.0, 0.0).astype(BF16)
        for j in range(width // LANES)
    ]
    return jnp.concatenate(parts, axis=1)


def with_ones(picked):
    lane = lax.broadcasted_iota(jnp.int32, picked.shape, 1)
    return jnp.where((lane >= DIM) & (lane < DIM + 3), 1.0, picked).astype(BF16)


def weigh(picked, coords):
    return jnp.exp2(dot_nt(with_ones(picked), coords) * SCALE)


def hi_lo(x):
    hi = x.astype(BF16)
    return hi, (x - hi.astype(F32)).astype(BF16)


def merge(both, chosen):
    rows = dot(one_hot(chosen, 2 * SKEL), both)
    picked = rows[:, :LANES]
    weights = weigh(picked, both[:, :LANES])
    totals = jnp.sum(weights, axis=1, keepdims=True)
    high, low = hi_lo(weights)
    mixed = dot(high, both[:, LANES:])
    mixed = mixed[:, :LANES] + mixed[:, LANES:] + dot(low, both[:, LANES : 2 * LANES])
    samples = rows[:, LANES : 2 * LANES] + rows[:, 2 * LANES :] + mixed / totals
    s_hi, s_lo = hi_lo(samples)
    return jnp.concatenate([picked.astype(BF16), s_hi, s_lo], axis=1), samples


def gather_kernel(
    leaf_count,
    points_ref,
    probes_ref,
    order_ref,
    sets_ref,
    merge_ref,
    probes_hbm,
    win_t,
    win_q,
    own_a,
    root_ref,
    own_t,
    own_c,
    nodes,
    pairs,
    tree,
    final,
    copy_sem,
    own_send,
    own_recv,
    fwd_send,
    fwd_recv,
    edge_send,
    edge_recv,
    tree_send,
    tree_recv,
):
    leaf = lax.axis_index("leaf")
    y = lax.axis_index("sub")
    rank = leaf * 4 + y
    first_block = rank * BLK
    plus = (leaf, lax.rem(y + 1, 4))
    minus = (leaf, lax.rem(y + 3, 4))
    up = (lax.rem(leaf + 1, leaf_count), y)
    down = (lax.rem(leaf + leaf_count - 1, leaf_count), y)
    levels = [("sub", d) for d in (1, 2)]
    d = 1
    while d < leaf_count:
        levels.append(("leaf", d))
        d *= 2

    def other(axis, dist):
        place = y if axis == "sub" else leaf
        bit = lax.rem(place // dist, 2)
        there = place + dist - 2 * dist * bit
        return bit, ((leaf, there) if axis == "sub" else (there, y))

    greet = [plus, minus, (leaf, lax.rem(y + 2, 4)), up, down]
    greet += [other(axis, dist)[1] for axis, dist in levels if axis == "leaf" and dist > 1]
    barrier = pltpu.get_barrier_semaphore()
    for who in greet:
        pl.semaphore_signal(barrier, inc=1, device_id=who, device_id_type=MESH)
    pl.semaphore_wait(barrier, len(greet))

    wins = (win_t, win_q)
    owns = (own_t, probes_hbm)

    def remote(src, dst, send, recv, who):
        return pltpu.make_async_remote_copy(
            src_ref=src, dst_ref=dst, send_sem=send, recv_sem=recv, device_id=who, device_id_type=MESH
        )

    def own_copy(kind, way, piece):
        at = (piece if way == 0 else 1 - piece) * HALF
        return remote(
            owns[kind].at[pl.ds(at, HALF)],
            wins[kind].at[pl.ds(BLK + y * BLK + at, HALF)],
            own_send.at[kind, way, piece],
            own_recv.at[kind, way, piece],
            plus if way == 0 else minus,
        )

    def fwd_copy(kind, way, j):
        src_y = lax.rem(y + 3, 4) if way == 0 else lax.rem(y + 1, 4)
        at = BLK + src_y * BLK + way * HALF + j
        ref = wins[kind].at[pl.ds(at, 1)]
        return remote(
            ref, ref, fwd_send.at[kind, way, j], fwd_recv.at[kind, way, j], plus if way == 0 else minus
        )

    def edge_copy(kind, side, j, own):
        at = (3 * BLK if side == 0 else 0) + j
        src = owns[kind].at[pl.ds(j, 1)] if own else wins[kind].at[pl.ds(BLK + at, 1)]
        return remote(
            src,
            wins[kind].at[pl.ds((0 if side == 0 else 5 * BLK) + j, 1)],
            edge_send.at[kind, side, j],
            edge_recv.at[kind, side, j],
            up if side == 0 else down,
        )

    has = (leaf < leaf_count - 1, leaf > 0)

    def start_edges(kind, j_from, j_to, prev_when, next_when, own=False):
        for side, cond in ((0, prev_when), (1, next_when)):

            @pl.when(cond & has[side])
            def _(side=side):
                def body(j, carry):
                    edge_copy(kind, side, j, own).start()
                    return carry

                lax.fori_loop(j_from, j_to, body, 0)

    for way in range(2):
        own_copy(1, way, 0).start()
    start_edges(1, 0, BLK, y == 3, y == 0, own=True)
    keep_q = pltpu.make_async_copy(probes_hbm, win_q.at[pl.ds(BLK + y * BLK, BLK)], copy_sem.at[1])
    keep_q.start()

    lane = lax.broadcasted_iota(jnp.int32, (LANES, LANES), 1)

    def permute(b, carry):
        pts = points_ref[pl.ds(b * LEAF, LEAF), :]
        pts = jnp.concatenate([pts, jnp.zeros((LEAF, LANES - DIM), BF16)], axis=1)
        for q in range(LEAF // LANES):
            hot = one_hot(order_ref[pl.ds(b * 4 + q, 1), :], LEAF)
            rows = dot(hot, pts)
            h1, h2, h3 = split3(-0.5 * jnp.sum(rows * rows, axis=1, keepdims=True))
            form = jnp.where(lane == DIM, h1, jnp.where(lane == DIM + 1, h2, jnp.where(lane == DIM + 2, h3, rows)))
            own_c[b, q * LANES : (q + 1) * LANES, :] = form.astype(BF16)
            ones = jnp.where((lane >= DIM + 3) & (lane < DIM + 6), 1.0, form)
            own_a[b, q * LANES : (q + 1) * LANES, :] = ones.astype(BF16)
            own_t[b, :, q * LANES : (q + 1) * LANES] = jnp.transpose(rows)[:DIM].astype(BF16)
        return carry

    lax.fori_loop(0, BLK, permute, 0)
    for way in range(2):
        own_copy(0, way, 0).start()
    start_edges(0, 0, BLK, y == 3, y == 0, own=True)
    keep_t = pltpu.make_async_copy(own_t, win_t.at[pl.ds(BLK + y * BLK, BLK)], copy_sem.at[0])
    keep_t.start()

    def leaf_node(b, carry):
        coords = own_c[b]
        probe = probes_ref[b]
        hot = one_hot(sets_ref[pl.ds(b, 1), :], LEAF)
        picked = dot(hot, coords)
        weights = weigh(picked, coords)
        totals = jnp.sum(weights, axis=1, keepdims=True)
        high, low = hi_lo(weights)
        samples = dot(hot, probe) + (dot(high, probe) + dot(low, probe)) / totals
        s_hi, s_lo = hi_lo(samples)
        nodes[pl.ds(pl.multiple_of(b * SKEL, SKEL), SKEL), :] = jnp.concatenate(
            [picked.astype(BF16), s_hi, s_lo], axis=1
        )
        return carry

    lax.fori_loop(0, BLK, leaf_node, 0)
    for way in range(2):
        for kind in range(2):
            own_copy(kind, way, 1).start()

    bit, _ = other(*levels[0])
    for k in range(4):
        chosen = merge_ref[pl.ds(first_block + 2 * k, 1), :]
        pairs[k * SKEL : (k + 1) * SKEL, :] = merge(nodes[2 * k * SKEL : 2 * (k + 1) * SKEL, :], chosen)[0]
    two = [
        merge(pairs[2 * k * SKEL : 2 * (k + 1) * SKEL, :], merge_ref[pl.ds(first_block + 4 * k + 1, 1), :])[0]
        for k in range(2)
    ]
    for k in range(2):
        nodes[k * SKEL : (k + 1) * SKEL, :] = two[k]
    node, samples = merge(nodes[: 2 * SKEL, :], merge_ref[pl.ds(first_block + 3, 1), :])

    def level(i, node):
        axis, dist = levels[i]
        bit, who = other(axis, dist)
        mine = pl.ds(pl.multiple_of(bit * SKEL, SKEL), SKEL)
        tree[i, mine, :] = node
        copy = remote(tree.at[i, mine], tree.at[i, mine], tree_send.at[i], tree_recv.at[i], who)
        copy.start()
        span = BLK * dist if axis == "sub" else BLK * 4 * dist
        first = first_block // (2 * span) * (2 * span)
        chosen = merge_ref[pl.ds(first + span - 1, 1), :]
        copy.wait()
        return merge(tree[i], chosen)

    near_prev = (y == 0) | (y == 2)
    near_next = (y == 1) | (y == 3)
    far_prev = y == 1
    far_next = y == 2
    from_minus = (y == 0, y == 1)
    from_plus = (y == 2, y == 3)

    node, samples = level(0, node)
    node, samples = level(1, node)
    for kind in (1, 0):
        for way in range(2):
            own_copy(kind, way, 0).wait_recv()

            def send_on(j, carry, kind=kind, way=way):
                fwd_copy(kind, way, j).start()
                return carry

            lax.fori_loop(0, HALF, send_on, 0)
        start_edges(kind, 0, HALF, *from_minus)
        start_edges(kind, HALF, BLK, *from_plus)
    half_way = 2 + (len(levels) - 2) // 2
    for i in range(2, half_way):
        node, samples = level(i, node)
    for kind in (1, 0):
        for way in range(2):
            own_copy(kind, way, 1).wait_recv()
        start_edges(kind, HALF, BLK, *from_minus)
        start_edges(kind, 0, HALF, *from_plus)
    for i in range(half_way, len(levels)):
        node, samples = level(i, node)
    final[...] = samples
    row = final[pl.ds(rank // 2, 1), :] if leaf_count == 64 else final[pl.ds(0, 1), :]
    odd = lax.rem(rank, 2) == 1
    row = jnp.broadcast_to(row, (8, LANES))
    root_ref[...] = jnp.where(odd, pltpu.roll(row, DIM, 1), row)

    def far(j, carry):
        for way in range(2):
            for kind in (1, 0):
                fwd_copy(kind, way, j).wait_recv()
                for side, cond in ((0, far_prev), (1, far_next)):

                    @pl.when(cond & has[side])
                    def _(side=side, kind=kind, way=way):
                        edge_copy(kind, side, way * HALF + j, False).start()

        return carry

    lax.fori_loop(0, HALF, far, 0)

    for kind in range(2):
        for way in range(2):
            for piece in range(2):
                own_copy(kind, way, piece).wait_send()

    def drain(j, carry):
        for kind in range(2):
            for way in range(2):
                fwd_copy(kind, way, j).wait_send()
        return carry

    lax.fori_loop(0, HALF, drain, 0)
    for side in range(2):

        @pl.when(has[side])
        def _(side=side):
            def body(j, carry):
                for kind in range(2):
                    edge_copy(kind, side, j, False).wait_send()
                return carry

            lax.fori_loop(0, BLK, body, 0)

        @pl.when(has[1 - side])
        def _(side=side):
            def body(j, carry):
                for kind in range(2):
                    edge_copy(kind, side, j, False).wait_recv()
                return carry

            lax.fori_loop(0, BLK, body, 0)

    keep_q.wait()
    keep_t.wait()


def near_kernel(
    lists_ref, counts_ref, own_a, win_t, win_q, out_ref, flat, ring_t, ring_q, acc, outs, sem_t, sem_q, sem_o
):
    start = lax.axis_index("leaf") * 32 - BLK

    def flatten(g, total):
        def one(s, carry):
            flat[total + s] = lists_ref[g, s] - start
            return carry

        count = counts_ref[g]
        lax.fori_loop(0, count, one, 0)
        return total + count

    total = lax.fori_loop(0, BLK, flatten, 0)

    def fetch(t):
        slot = lax.rem(t, RING)
        c = flat[t]
        return (
            pltpu.make_async_copy(win_t.at[c], ring_t.at[slot, pl.ds(0, DIM)], sem_t.at[slot]),
            pltpu.make_async_copy(win_q.at[c], ring_q.at[slot], sem_q.at[slot]),
        )

    def begin(t, carry):
        for copy in fetch(t):
            copy.start()
        return carry

    lax.fori_loop(0, jnp.minimum(total, RING - 1), begin, 0)
    for slot in range(RING):
        ring_t[slot, DIM:, :] = jnp.zeros((LANES - DIM, LEAF), BF16)
    row_id = lax.broadcasted_iota(jnp.int32, (16, LEAF), 0)

    def block(g, t0):
        acc[...] = jnp.zeros_like(acc)

        def pair(s, carry):
            t = t0 + s
            slot = lax.rem(t, RING)

            @pl.when(t + RING - 1 < total)
            def _():
                for copy in fetch(t + RING - 1):
                    copy.start()

            for copy in fetch(t):
                copy.wait()
            pts = ring_t[slot, :DIM, :].astype(F32)
            h1, h2, h3 = split3(-0.5 * jnp.sum(pts * pts, axis=0, keepdims=True))
            tail = jnp.where(row_id < 3, 1.0, 0.0)
            tail = jnp.where(row_id == 3, h1, jnp.where(row_id == 4, h2, jnp.where(row_id == 5, h3, tail)))
            ring_t[slot, DIM : DIM + 16, :] = tail.astype(BF16)
            source = ring_t[slot]
            probe = ring_q[slot]
            for q in range(LEAF // LANES):
                rows = slice(q * LANES, (q + 1) * LANES)
                weights = jnp.exp2(dot(own_a[g, rows, :], source) * SCALE).astype(BF16)
                acc[rows, :] += dot(weights, probe)
            return carry

        count = counts_ref[g]
        lax.fori_loop(0, count, pair, 0)
        which = lax.rem(g, 2)
        done = pltpu.make_async_copy(outs.at[which], out_ref.at[g], sem_o.at[which])

        @pl.when(g >= 2)
        def _():
            done.wait()

        outs[which] = acc[...] * (LEAF**-0.5)
        done.start()
        return t0 + count

    lax.fori_loop(0, BLK, block, 0)
    for g in (BLK - 2, BLK - 1):
        pltpu.make_async_copy(outs.at[g % 2], out_ref.at[g], sem_o.at[g % 2]).wait()


def on_device(points, probes, order, near_lists, near_counts, leaf_sets, merge_sets):
    leaf_count = lax.axis_size("leaf")
    vmem = pl.BlockSpec(memory_space=pltpu.VMEM)
    hbm = pl.BlockSpec(memory_space=pltpu.HBM)
    smem = pl.BlockSpec(memory_space=pltpu.SMEM)
    window = 6 * BLK
    level_count = 2 + leaf_count.bit_length() - 1
    probe_blocks = probes.reshape(BLK, LEAF, LANES)
    dma = pltpu.SemaphoreType.DMA
    win_t, win_q, own_a, root = pl.pallas_call(
        functools.partial(gather_kernel, leaf_count),
        out_shape=(
            jax.ShapeDtypeStruct((window, DIM, LEAF), BF16),
            jax.ShapeDtypeStruct((window, LEAF, LANES), BF16),
            jax.ShapeDtypeStruct((BLK, LEAF, LANES), BF16),
            jax.ShapeDtypeStruct((8, LANES), F32),
        ),
        in_specs=[vmem, vmem, vmem, vmem, vmem, hbm],
        out_specs=(hbm, hbm, vmem, vmem),
        scratch_shapes=[
            pltpu.VMEM((BLK, DIM, LEAF), BF16),
            pltpu.VMEM((BLK, LEAF, LANES), BF16),
            pltpu.VMEM((BLK * SKEL, 3 * LANES), BF16),
            pltpu.VMEM((BLK // 2 * SKEL, 3 * LANES), BF16),
            pltpu.VMEM((level_count, 2 * SKEL, 3 * LANES), BF16),
            pltpu.VMEM((SKEL, LANES), F32),
            dma((2,)),
            dma((2, 2, 2)),
            dma((2, 2, 2)),
            dma((2, 2, HALF)),
            dma((2, 2, HALF)),
            dma((2, 2, BLK)),
            dma((2, 2, BLK)),
            dma((level_count,)),
            dma((level_count,)),
        ],
        compiler_params=pltpu.CompilerParams(
            collective_id=0, has_side_effects=True, vmem_limit_bytes=40 * 2**20
        ),
        name="gather_and_tree",
    )(points, probe_blocks, order.reshape(-1, LANES), leaf_sets, merge_sets, probe_blocks)
    near = pl.pallas_call(
        near_kernel,
        out_shape=jax.ShapeDtypeStruct((BLK, LEAF, LANES), F32),
        in_specs=[smem, smem, vmem, hbm, hbm],
        out_specs=hbm,
        scratch_shapes=[
            pltpu.SMEM((128,), jnp.int32),
            pltpu.VMEM((RING, LANES, LEAF), BF16),
            pltpu.VMEM((RING, LEAF, LANES), BF16),
            pltpu.VMEM((LEAF, LANES), F32),
            pltpu.VMEM((2, LEAF, LANES), F32),
            dma((RING,)),
            dma((RING,)),
            dma((2,)),
        ],
        compiler_params=pltpu.CompilerParams(vmem_limit_bytes=40 * 2**20),
        name="near_field",
    )(near_lists, near_counts, own_a, win_t, win_q)
    return near.reshape(BLK * LEAF, LANES), root[0, :DIM]


def solution(mesh):
    both = P(("leaf", "sub"), None)
    in_specs = (both, both, P(("leaf", "sub")), both, P(("leaf", "sub")), both, P())
    out_specs = (both, P(("leaf", "sub")))
    return jax.shard_map(on_device, mesh=mesh, in_specs=in_specs, out_specs=out_specs, check_vma=False)
```

```python
import functools

import jax
import jax.numpy as jnp
from jax import lax
from jax.experimental import pallas as pl
from jax.experimental.pallas import tpu as pltpu
from jax.sharding import PartitionSpec as P

MESH = pl.DeviceIdType.MESH
BF16 = jnp.bfloat16
F32 = jnp.float32
LANES = 128
LEAF = 512
DIM = 64
FORM = DIM + 16
BLK = 8
HALF = 4
SKEL = 128
NODE = FORM + 2 * SKEL
PAIRS = 4
LOG2E = 1.4426950408889634
SCALE = 2.0 * LOG2E / DIM


def dot(a, b):
    return jnp.dot(a, b, preferred_element_type=F32)


def dot_tn(a, b):
    return lax.dot_general(a, b, (((0,), (0,)), ((), ())), preferred_element_type=F32)


def half_squares(coords):
    h = -0.5 * jnp.sum(coords * coords, axis=0, keepdims=True)
    h1 = h.astype(BF16).astype(F32)
    h2 = (h - h1).astype(BF16).astype(F32)
    h3 = (h - h1 - h2).astype(BF16).astype(F32)
    return h1, h2, h3


def tail_rows(squares, first, ones):
    shape = (FORM - DIM, squares[0].shape[1])
    row = lax.broadcasted_iota(jnp.int32, shape, 0)
    tail = jnp.zeros(shape, F32)
    if ones is not None:
        tail = jnp.where((row >= ones) & (row < ones + 3), 1.0, tail)
    for i, part in enumerate(squares):
        tail = jnp.where(row == first + i, part, tail)
    return tail.astype(BF16)


def one_hot(row, height):
    shape = (height, row.shape[1])
    return jnp.where(lax.broadcasted_iota(jnp.int32, shape, 0) == row, 1.0, 0.0).astype(BF16)


def weigh(picked, coords):
    row = lax.broadcasted_iota(jnp.int32, picked.shape, 0)
    left = jnp.where((row >= DIM) & (row < DIM + 3), 1.0, picked).astype(BF16)
    return jnp.exp2(dot_tn(left, coords) * SCALE)


def hi_lo(x):
    hi = x.astype(BF16)
    return hi, (x - hi.astype(F32)).astype(BF16)


def node_of(picked, samples):
    return jnp.concatenate([picked.astype(BF16), *hi_lo(samples)], axis=0)


def merge(left, right, chosen):
    coords = jnp.concatenate([left[:FORM], right[:FORM]], axis=1)
    high = jnp.concatenate([left[FORM : FORM + SKEL], right[FORM : FORM + SKEL]], axis=0)
    low = jnp.concatenate([left[FORM + SKEL :], right[FORM + SKEL :]], axis=0)
    both = jnp.concatenate([high, low], axis=1)
    hot = one_hot(chosen, 2 * SKEL)
    picked = dot(coords, hot)
    kept = dot_tn(hot, both)
    weights = weigh(picked, coords)
    totals = jnp.sum(weights, axis=1, keepdims=True)
    w_hi, w_lo = hi_lo(weights)
    mixed = dot(w_hi, both)
    mixed = mixed[:, :LANES] + mixed[:, LANES:] + dot(w_lo, high)
    samples = kept[:, :LANES] + kept[:, LANES:] + mixed / totals
    return picked, samples


def gather_kernel(
    leaf_count,
    points_hbm,
    probes_hbm,
    order_hbm,
    sets_hbm,
    merge_hbm,
    win_t,
    win_q,
    root_ref,
    points,
    order,
    sets,
    chosen_rows,
    own_h,
    nodes,
    tree,
    final,
    in_sem,
    row_sem,
    own_send,
    own_recv,
    fwd_send,
    fwd_recv,
    edge_send,
    edge_recv,
    tree_send,
    tree_recv,
):
    leaf = lax.axis_index("leaf")
    y = lax.axis_index("sub")
    rank = leaf * 4 + y
    first_block = rank * BLK
    mine = BLK + y * BLK
    plus = (leaf, lax.rem(y + 1, 4))
    minus = (leaf, lax.rem(y + 3, 4))
    up = (lax.rem(leaf + 1, leaf_count), y)
    down = (lax.rem(leaf + leaf_count - 1, leaf_count), y)
    levels = [("sub", d) for d in (1, 2)]
    d = 1
    while d < leaf_count:
        levels.append(("leaf", d))
        d *= 2

    def other(axis, dist):
        place = y if axis == "sub" else leaf
        bit = lax.rem(place // dist, 2)
        there = place + dist - 2 * dist * bit
        return bit, ((leaf, there) if axis == "sub" else (there, y))

    inputs = [
        pltpu.make_async_copy(order_hbm, order, in_sem.at[0]),
        pltpu.make_async_copy(points_hbm, points, in_sem.at[1]),
        pltpu.make_async_copy(sets_hbm, sets, in_sem.at[2]),
        pltpu.make_async_copy(probes_hbm, win_q.at[pl.ds(mine, BLK)], in_sem.at[3]),
    ]
    wanted = [first_block + i for i in range(7)]
    for axis, dist in levels:
        span = BLK * dist if axis == "sub" else BLK * 4 * dist
        wanted.append(first_block // (2 * span) * (2 * span) + span - 1)
    rows = [
        pltpu.make_async_copy(merge_hbm.at[pl.ds(w, 1)], chosen_rows.at[pl.ds(i, 1)], row_sem.at[i])
        for i, w in enumerate(wanted)
    ]
    for copy in inputs + rows:
        copy.start()

    greet = [plus, minus, (leaf, lax.rem(y + 2, 4)), up, down]
    greet += [other(axis, dist)[1] for axis, dist in levels if axis == "leaf" and dist > 1]
    barrier = pltpu.get_barrier_semaphore()
    for who in greet:
        pl.semaphore_signal(barrier, inc=1, device_id=who, device_id_type=MESH)
    pl.semaphore_wait(barrier, len(greet))

    wins = (win_t, win_q)

    def remote(src, dst, send, recv, who):
        return pltpu.make_async_remote_copy(
            src_ref=src, dst_ref=dst, send_sem=send, recv_sem=recv, device_id=who, device_id_type=MESH
        )

    def own_copy(kind, way, piece):
        at = (piece if way == 0 else 1 - piece) * HALF
        there = wins[kind].at[pl.ds(mine + at, HALF)]
        return remote(
            probes_hbm.at[pl.ds(at, HALF)] if kind else there,
            there,
            own_send.at[kind, way, piece],
            own_recv.at[kind, way, piece],
            plus if way == 0 else minus,
        )

    def fwd_copy(kind, way, j):
        src_y = lax.rem(y + 3, 4) if way == 0 else lax.rem(y + 1, 4)
        ref = wins[kind].at[pl.ds(BLK + src_y * BLK + way * HALF + j, 1)]
        return remote(
            ref, ref, fwd_send.at[kind, way, j], fwd_recv.at[kind, way, j], plus if way == 0 else minus
        )

    def edge_copy(kind, side, j, own=False):
        at = BLK + (3 * BLK if side == 0 else 0) + j
        src = probes_hbm.at[pl.ds(j, 1)] if own and kind else wins[kind].at[pl.ds(at, 1)]
        return remote(
            src,
            wins[kind].at[pl.ds((0 if side == 0 else 5 * BLK) + j, 1)],
            edge_send.at[kind, side, j],
            edge_recv.at[kind, side, j],
            up if side == 0 else down,
        )

    has = (leaf < leaf_count - 1, leaf > 0)

    def start_edges(kind, j_from, j_to, prev_when, next_when, own=False):
        for side, cond in ((0, prev_when), (1, next_when)):

            @pl.when(cond & has[side])
            def _(side=side):
                def body(j, carry):
                    edge_copy(kind, side, j, own).start()
                    return carry

                lax.fori_loop(j_from, j_to, body, 0)

    for way in range(2):
        own_copy(1, way, 0).start()
    start_edges(1, 0, BLK, y == 3, y == 0, own=True)

    inputs[0].wait()
    inputs[1].wait()

    def permute(i, carry):
        for k in range(2):
            b = 2 * i + k
            to = jnp.concatenate([order[pl.ds(b * 4 + q, 1), :] for q in range(4)], axis=1)
            at = pl.ds(pl.multiple_of(b * LEAF, LEAF), LEAF)
            coords = dot(points[:, at], one_hot(to, LEAF))
            win_t[mine + b] = coords.astype(BF16)
            own_h[b] = tail_rows(half_squares(coords), 0, None)
        return carry

    lax.fori_loop(0, BLK // 2, permute, 0)
    for way in range(2):
        own_copy(0, way, 0).start()
    start_edges(0, 0, BLK, y == 3, y == 0, own=True)

    inputs[2].wait()
    inputs[3].wait()

    def leaf_nodes(i, carry):
        for k in range(4):
            b = 4 * i + k
            coords = jnp.concatenate([win_t[mine + b], own_h[b]], axis=0)
            probe = win_q[mine + b]
            hot = one_hot(sets[pl.ds(b, 1), :], LEAF)
            picked = dot(coords, hot)
            kept = dot_tn(hot, probe)
            weights = weigh(picked, coords)
            totals = jnp.sum(weights, axis=1, keepdims=True)
            w_hi, w_lo = hi_lo(weights)
            samples = kept + (dot(w_hi, probe) + dot(w_lo, probe)) / totals
            nodes[b] = node_of(picked, samples)
        return carry

    lax.fori_loop(0, BLK // 4, leaf_nodes, 0)
    for way in range(2):
        own_copy(1, way, 1).start()
    for copy in rows:
        copy.wait()

    def row(i):
        return chosen_rows[i : i + 1, :]

    def merge_all(count, first, step):
        out = [node_of(*merge(nodes[2 * k], nodes[2 * k + 1], row(first + step * k))) for k in range(count)]
        for k in range(count):
            nodes[k] = out[k]

    merge_all(4, 0, 2)
    merge_all(2, 1, 4)
    picked, samples = merge(nodes[0], nodes[1], row(3))

    def level(i, picked, samples):
        axis, dist = levels[i]
        bit, who = other(axis, dist)
        tree[i, bit] = node_of(picked, samples)
        ref = tree.at[i, bit]
        copy = remote(ref, ref, tree_send.at[i], tree_recv.at[i], who)
        copy.start()
        copy.wait()
        return merge(tree[i, 0], tree[i, 1], row(7 + i))

    far_prev = y == 1
    far_next = y == 2
    from_minus = (y == 0, y == 1)
    from_plus = (y == 2, y == 3)

    for i in range(2):
        picked, samples = level(i, picked, samples)
    for kind in (1, 0):
        for way in range(2):
            own_copy(kind, way, 0).wait_recv()

            def send_on(j, carry, kind=kind, way=way):
                fwd_copy(kind, way, j).start()
                return carry

            lax.fori_loop(0, HALF, send_on, 0)
        start_edges(kind, 0, HALF, *from_minus)
        start_edges(kind, HALF, BLK, *from_plus)
    for way in range(2):
        own_copy(0, way, 1).start()
    half_way = 2 + (len(levels) - 2) * 2 // 3
    for i in range(2, half_way):
        picked, samples = level(i, picked, samples)
    for kind in (1, 0):
        for way in range(2):
            own_copy(kind, way, 1).wait_recv()
        start_edges(kind, HALF, BLK, *from_minus)
        start_edges(kind, 0, HALF, *from_plus)
    for i in range(half_way, len(levels)):
        picked, samples = level(i, picked, samples)
    final[...] = samples
    last = final[pl.ds(rank // 2 if leaf_count == 64 else 0, 1), :]
    last = jnp.broadcast_to(last, (8, LANES))
    root_ref[...] = jnp.where(lax.rem(rank, 2) == 1, pltpu.roll(last, DIM, 1), last)

    def far(j, carry):
        for way in range(2):
            for kind in (1, 0):
                fwd_copy(kind, way, j).wait_recv()
                for side, cond in ((0, far_prev), (1, far_next)):

                    @pl.when(cond & has[side])
                    def _(side=side, kind=kind, way=way):
                        edge_copy(kind, side, way * HALF + j).start()

        return carry

    lax.fori_loop(0, HALF, far, 0)

    for kind in range(2):
        for way in range(2):
            for piece in range(2):
                own_copy(kind, way, piece).wait_send()

    def drain(j, carry):
        for kind in range(2):
            for way in range(2):
                fwd_copy(kind, way, j).wait_send()
        return carry

    lax.fori_loop(0, HALF, drain, 0)
    for side in range(2):

        @pl.when(has[side])
        def _(side=side):
            def body(j, carry):
                for kind in range(2):
                    edge_copy(kind, side, j).wait_send()
                return carry

            lax.fori_loop(0, BLK, body, 0)

        @pl.when(has[1 - side])
        def _(side=side):
            def body(j, carry):
                for kind in range(2):
                    edge_copy(kind, side, j).wait_recv()
                return carry

            lax.fori_loop(0, BLK, body, 0)


def near_kernel(lists_ref, counts_ref, win_t, win_q, out_ref, flat_g, flat_c, acc, outs, sem_o):
    start = lax.axis_index("leaf") * 32 - BLK
    mine = BLK + lax.axis_index("sub") * BLK

    def flatten(g, total):
        def one(s, carry):
            flat_g[total + s] = g
            flat_c[total + s] = lists_ref[g, s] - start
            return carry

        count = counts_ref[g]
        lax.fori_loop(0, count, one, 0)
        return total + count

    total = lax.fori_loop(0, BLK, flatten, 0)
    for i in range(PAIRS - 1):
        flat_g[total + i] = BLK
        flat_c[total + i] = mine
    acc[...] = jnp.zeros_like(acc)

    def step(i, carry):
        for k in range(PAIRS):
            g = flat_g[i * PAIRS + k]
            c = flat_c[i * PAIRS + k]
            target = win_t[mine + jnp.minimum(g, BLK - 1)]
            source = win_t[c]
            left = jnp.concatenate([target, tail_rows(half_squares(target.astype(F32)), 0, 3)], axis=0)
            right = jnp.concatenate([source, tail_rows(half_squares(source.astype(F32)), 3, 0)], axis=0)
            weights = jnp.exp2(dot_tn(left, right) * SCALE).astype(BF16)
            acc[g] += dot(weights, win_q[c])
        return carry

    lax.fori_loop(0, (total + PAIRS - 1) // PAIRS, step, 0)
    for g in range(BLK):
        outs[g] = acc[g] * (LEAF**-0.5)
        pltpu.make_async_copy(outs.at[g], out_ref.at[g], sem_o.at[g]).start()
    for g in range(BLK):
        pltpu.make_async_copy(outs.at[g], out_ref.at[g], sem_o.at[g]).wait()


def in_hbm(x):
    return pltpu.with_memory_space_constraint(x, pltpu.HBM)


def on_device(points, probes, order, near_lists, near_counts, leaf_sets, merge_sets):
    leaf_count = lax.axis_size("leaf")
    vmem = pl.BlockSpec(memory_space=pltpu.VMEM)
    hbm = pl.BlockSpec(memory_space=pltpu.HBM)
    smem = pl.BlockSpec(memory_space=pltpu.SMEM)
    window = 6 * BLK
    level_count = 2 + leaf_count.bit_length() - 1
    dma = pltpu.SemaphoreType.DMA
    win_t, win_q, root = pl.pallas_call(
        functools.partial(gather_kernel, leaf_count),
        out_shape=(
            jax.ShapeDtypeStruct((window, DIM, LEAF), BF16),
            jax.ShapeDtypeStruct((window, LEAF, LANES), BF16),
            jax.ShapeDtypeStruct((8, LANES), F32),
        ),
        in_specs=[hbm] * 5,
        out_specs=(vmem, vmem, vmem),
        scratch_shapes=[
            pltpu.VMEM((DIM, BLK * LEAF), BF16),
            pltpu.VMEM((BLK * LEAF // LANES, LANES), jnp.int32),
            pltpu.VMEM((BLK, SKEL), jnp.int32),
            pltpu.VMEM((16, SKEL), jnp.int32),
            pltpu.VMEM((BLK, FORM - DIM, LEAF), BF16),
            pltpu.VMEM((BLK, NODE, LANES), BF16),
            pltpu.VMEM((level_count, 2, NODE, LANES), BF16),
            pltpu.VMEM((SKEL, LANES), F32),
            dma((4,)),
            dma((7 + level_count,)),
            dma((2, 2, 2)),
            dma((2, 2, 2)),
            dma((2, 2, HALF)),
            dma((2, 2, HALF)),
            dma((2, 2, BLK)),
            dma((2, 2, BLK)),
            dma((level_count,)),
            dma((level_count,)),
        ],
        compiler_params=pltpu.CompilerParams(
            collective_id=0, has_side_effects=True, vmem_limit_bytes=32 * 2**20
        ),
        name="gather_and_tree",
    )(*map(in_hbm, (points.T, probes.reshape(BLK, LEAF, LANES), order.reshape(-1, LANES), leaf_sets, merge_sets)))
    near = pl.pallas_call(
        near_kernel,
        out_shape=jax.ShapeDtypeStruct((BLK, LEAF, LANES), F32),
        in_specs=[smem, smem, vmem, vmem],
        out_specs=hbm,
        scratch_shapes=[
            pltpu.SMEM((128,), jnp.int32),
            pltpu.SMEM((128,), jnp.int32),
            pltpu.VMEM((BLK + 1, LEAF, LANES), F32),
            pltpu.VMEM((BLK, LEAF, LANES), F32),
            dma((BLK,)),
        ],
        compiler_params=pltpu.CompilerParams(vmem_limit_bytes=32 * 2**20),
        name="near_field",
    )(in_hbm(near_lists), in_hbm(near_counts), win_t, win_q)
    return near.reshape(BLK * LEAF, LANES), root[0, :DIM]


def solution(mesh):
    both = P(("leaf", "sub"), None)
    in_specs = (both, both, P(("leaf", "sub")), both, P(("leaf", "sub")), both, P())
    out_specs = (both, P(("leaf", "sub")))
    return jax.shard_map(on_device, mesh=mesh, in_specs=in_specs, out_specs=out_specs, check_vma=False)
```

```python
import functools

import jax
import jax.numpy as jnp
from jax import lax
from jax.experimental import pallas as pl
from jax.experimental.pallas import tpu as pltpu
from jax.sharding import PartitionSpec as P

MESH = pl.DeviceIdType.MESH
BF16 = jnp.bfloat16
F32 = jnp.float32
LANES = 128
LEAF = 512
DIM = 64
FORM = DIM + 16
BLK = 8
HALF = 4
SKEL = 128
NODE = FORM + 2 * SKEL
PAIRS = 8
LOG2E = 1.4426950408889634
SCALE = 2.0 * LOG2E / DIM


def dot(a, b):
    return jnp.dot(a, b, preferred_element_type=F32)


def dot_tn(a, b):
    return lax.dot_general(a, b, (((0,), (0,)), ((), ())), preferred_element_type=F32)


def half_squares(coords):
    h = -0.5 * jnp.sum(coords * coords, axis=0, keepdims=True)
    h1 = h.astype(BF16).astype(F32)
    h2 = (h - h1).astype(BF16).astype(F32)
    h3 = (h - h1 - h2).astype(BF16).astype(F32)
    return h1, h2, h3


def tail_rows(squares, first, ones):
    shape = (FORM - DIM, squares[0].shape[1])
    row = lax.broadcasted_iota(jnp.int32, shape, 0)
    tail = jnp.zeros(shape, F32)
    if ones is not None:
        tail = jnp.where((row >= ones) & (row < ones + 3), 1.0, tail)
    for i, part in enumerate(squares):
        tail = jnp.where(row == first + i, part, tail)
    return tail.astype(BF16)


def one_hot(row, height):
    shape = (height, row.shape[1])
    return jnp.where(lax.broadcasted_iota(jnp.int32, shape, 0) == row, 1.0, 0.0).astype(BF16)


def weigh(picked, coords):
    row = lax.broadcasted_iota(jnp.int32, picked.shape, 0)
    left = jnp.where((row >= DIM) & (row < DIM + 3), 1.0, picked).astype(BF16)
    return jnp.exp2(dot_tn(left, coords) * SCALE)


def hi_lo(x):
    hi = x.astype(BF16)
    return hi, (x - hi.astype(F32)).astype(BF16)


def node_of(picked, samples):
    return jnp.concatenate([picked.astype(BF16), *hi_lo(samples)], axis=0)


def merge(left, right, chosen):
    coords = jnp.concatenate([left[:FORM], right[:FORM]], axis=1)
    high = jnp.concatenate([left[FORM : FORM + SKEL], right[FORM : FORM + SKEL]], axis=0)
    low = jnp.concatenate([left[FORM + SKEL :], right[FORM + SKEL :]], axis=0)
    both = jnp.concatenate([high, low], axis=1)
    hot = one_hot(chosen, 2 * SKEL)
    picked = dot(coords, hot)
    kept = dot_tn(hot, both)
    weights = weigh(picked, coords)
    totals = jnp.sum(weights, axis=1, keepdims=True)
    w_hi, w_lo = hi_lo(weights)
    mixed = dot(w_hi, both)
    mixed = mixed[:, :LANES] + mixed[:, LANES:] + dot(w_lo, high)
    samples = kept[:, :LANES] + kept[:, LANES:] + mixed / totals
    return picked, samples


def rounds_of(leaf_count):
    rounds = [("sub", 1, 4), ("leaf", 1, 2)]
    d = 2
    while d < leaf_count:
        rounds.append(("leaf", d, 4 if 4 * d <= leaf_count else 2))
        d *= rounds[-1][2]
    return rounds


def gather_kernel(
    leaf_count,
    points_hbm,
    probes_hbm,
    order_hbm,
    sets_hbm,
    merge_hbm,
    win_t,
    win_q,
    root_ref,
    points,
    order,
    sets,
    chosen_rows,
    own_h,
    nodes,
    tree,
    final,
    in_sem,
    row_sem,
    own_send,
    own_recv,
    late_send,
    late_recv,
    fwd_send,
    fwd_recv,
    edge_send,
    edge_recv,
    tree_send,
    tree_recv,
):
    leaf = lax.axis_index("leaf")
    y = lax.axis_index("sub")
    rank = leaf * 4 + y
    first_block = rank * BLK
    mine = BLK + y * BLK
    plus = (leaf, lax.rem(y + 1, 4))
    minus = (leaf, lax.rem(y + 3, 4))
    up = (lax.rem(leaf + 1, leaf_count), y)
    down = (lax.rem(leaf + leaf_count - 1, leaf_count), y)
    rounds = rounds_of(leaf_count)

    def partner(axis, d, n, k):
        place = y if axis == "sub" else leaf
        me = lax.rem(place // d, n)
        there = place + (lax.rem(me + k, n) - me) * d
        return me, ((leaf, there) if axis == "sub" else (there, y))

    inputs = [
        pltpu.make_async_copy(order_hbm, order, in_sem.at[0]),
        pltpu.make_async_copy(points_hbm, points, in_sem.at[1]),
        pltpu.make_async_copy(sets_hbm, sets, in_sem.at[2]),
        pltpu.make_async_copy(probes_hbm, win_q.at[pl.ds(mine, BLK)], in_sem.at[3]),
    ]
    wanted = [first_block + i for i in range(7)]
    row_at = []
    for axis, d, n in rounds:
        span = BLK * d if axis == "sub" else BLK * 4 * d
        first = first_block // (n * span) * (n * span)
        row_at.append(len(wanted))
        wanted += [first + span - 1] if n == 2 else [first + span - 1, first + 3 * span - 1, first + 2 * span - 1]
    rows = [
        pltpu.make_async_copy(merge_hbm.at[pl.ds(w, 1)], chosen_rows.at[pl.ds(i, 1)], row_sem.at[i])
        for i, w in enumerate(wanted)
    ]
    for copy in inputs + rows:
        copy.start()

    greet = [up, down]
    for axis, d, n in rounds:
        if axis == "sub" or d > 1:
            greet += [partner(axis, d, n, k)[1] for k in range(1, n)]
    barrier = pltpu.get_barrier_semaphore()
    for who in greet:
        pl.semaphore_signal(barrier, inc=1, device_id=who, device_id_type=MESH)
    pl.semaphore_wait(barrier, len(greet))

    wins = (win_t, win_q)

    def remote(src, dst, send, recv, who):
        return pltpu.make_async_remote_copy(
            src_ref=src, dst_ref=dst, send_sem=send, recv_sem=recv, device_id=who, device_id_type=MESH
        )

    def own_piece(kind, way, at, size, send, recv):
        there = wins[kind].at[pl.ds(mine + at, size)]
        src = probes_hbm.at[pl.ds(at, size)] if kind else there
        return remote(src, there, send, recv, plus if way == 0 else minus)

    def early(kind, way):
        return own_piece(kind, way, way * HALF, HALF, own_send.at[kind, way], own_recv.at[kind, way])

    def late(kind, way, p):
        at = (1 - way) * HALF + 2 * p
        return own_piece(kind, way, at, 2, late_send.at[kind, way, p], late_recv.at[kind, way, p])

    def fwd_copy(kind, way, j):
        src_y = lax.rem(y + 3, 4) if way == 0 else lax.rem(y + 1, 4)
        ref = wins[kind].at[pl.ds(BLK + src_y * BLK + way * HALF + j, 1)]
        return remote(
            ref, ref, fwd_send.at[kind, way, j], fwd_recv.at[kind, way, j], plus if way == 0 else minus
        )

    def edge_copy(kind, side, j, own=False):
        at = BLK + (3 * BLK if side == 0 else 0) + j
        src = probes_hbm.at[pl.ds(j, 1)] if own and kind else wins[kind].at[pl.ds(at, 1)]
        return remote(
            src,
            wins[kind].at[pl.ds((0 if side == 0 else 5 * BLK) + j, 1)],
            edge_send.at[kind, side, j],
            edge_recv.at[kind, side, j],
            up if side == 0 else down,
        )

    has = (leaf < leaf_count - 1, leaf > 0)

    def start_edges(kinds, j_from, j_to, prev_when, next_when, own=False):
        for side, cond in ((0, prev_when), (1, next_when)):

            @pl.when(cond & has[side])
            def _(side=side):
                def body(j, carry):
                    for kind in kinds:
                        edge_copy(kind, side, j, own).start()
                    return carry

                lax.fori_loop(j_from, j_to, body, 0)

    for way in range(2):
        early(1, way).start()
    start_edges((1,), 0, BLK, y == 3, y == 0, own=True)

    inputs[0].wait()
    inputs[1].wait()

    def permute(i, carry):
        for k in range(2):
            b = 2 * i + k
            to = jnp.concatenate([order[pl.ds(b * 4 + q, 1), :] for q in range(4)], axis=1)
            at = pl.ds(pl.multiple_of(b * LEAF, LEAF), LEAF)
            coords = dot(points[:, at], one_hot(to, LEAF))
            win_t[mine + b] = coords.astype(BF16)
            own_h[b] = tail_rows(half_squares(coords), 0, None)
        return carry

    lax.fori_loop(0, BLK // 2, permute, 0)
    for way in range(2):
        early(0, way).start()
    start_edges((0,), 0, BLK, y == 3, y == 0, own=True)

    inputs[2].wait()
    inputs[3].wait()

    def leaf_nodes(i, carry):
        for k in range(4):
            b = 4 * i + k
            coords = jnp.concatenate([win_t[mine + b], own_h[b]], axis=0)
            probe = win_q[mine + b]
            hot = one_hot(sets[pl.ds(b, 1), :], LEAF)
            picked = dot(coords, hot)
            kept = dot_tn(hot, probe)
            weights = weigh(picked, coords)
            totals = jnp.sum(weights, axis=1, keepdims=True)
            w_hi, w_lo = hi_lo(weights)
            samples = kept + (dot(w_hi, probe) + dot(w_lo, probe)) / totals
            nodes[b] = node_of(picked, samples)
        return carry

    lax.fori_loop(0, BLK // 4, leaf_nodes, 0)
    for copy in rows:
        copy.wait()

    def row(i):
        return chosen_rows[i : i + 1, :]

    def merge_all(count, first, step):
        out = [node_of(*merge(nodes[2 * k], nodes[2 * k + 1], row(first + step * k))) for k in range(count)]
        for k in range(count):
            nodes[k] = out[k]

    merge_all(4, 0, 2)
    merge_all(2, 1, 4)
    state = merge(nodes[0], nodes[1], row(3))

    def begin(i, state):
        axis, d, n = rounds[i]
        me, _ = partner(axis, d, n, 1)
        ref = tree.at[i, me]
        tree[i, me] = node_of(*state)
        copies = [
            remote(ref, ref, tree_send.at[i, k - 1], tree_recv.at[i, k - 1], partner(axis, d, n, k)[1])
            for k in range(1, n)
        ]
        for copy in copies:
            copy.start()
        return copies

    def finish(i, copies):
        for copy in copies:
            copy.wait()
        at = row_at[i]
        if rounds[i][2] == 2:
            return merge(tree[i, 0], tree[i, 1], row(at))
        low = node_of(*merge(tree[i, 0], tree[i, 1], row(at)))
        high = node_of(*merge(tree[i, 2], tree[i, 3], row(at + 1)))
        return merge(low, high, row(at + 2))

    from_minus = (y == 0, y == 1)
    from_plus = (y == 2, y == 3)

    copies = begin(0, state)
    for kind in (1, 0):
        for way in range(2):
            early(kind, way).wait_recv()

    def send_on(j, carry):
        for way in range(2):
            for kind in (1, 0):
                fwd_copy(kind, way, j).start()
        return carry

    lax.fori_loop(0, HALF, send_on, 0)
    start_edges((1, 0), 0, HALF, *from_minus)
    start_edges((1, 0), HALF, BLK, *from_plus)
    for p in range(2):
        for way in range(2):
            for kind in (1, 0):
                late(kind, way, p).start()
    state = finish(0, copies)

    def far(j, carry):
        for way in range(2):
            for kind in (1, 0):
                fwd_copy(kind, way, j).wait_recv()
        for side, cond in ((0, y == 1), (1, y == 2)):

            @pl.when(cond & has[side])
            def _(side=side):
                for way in range(2):
                    for kind in (1, 0):
                        edge_copy(kind, side, way * HALF + j).start()

        return carry

    for i in range(1, len(rounds)):
        copies = begin(i, state)
        if i == len(rounds) - 2:
            lax.fori_loop(0, HALF // 2, far, 0)
        if i == len(rounds) - 1:
            lax.fori_loop(HALF // 2, HALF, far, 0)
        state = finish(i, copies)
    final[...] = state[1]
    last = final[pl.ds(rank // 2 if leaf_count == 64 else 0, 1), :]
    last = jnp.broadcast_to(last, (8, LANES))
    root_ref[...] = jnp.where(lax.rem(rank, 2) == 1, pltpu.roll(last, DIM, 1), last)

    for p in range(2):
        for way in range(2):
            for kind in (1, 0):
                late(kind, way, p).wait_recv()
        start_edges((1, 0), HALF + 2 * p, HALF + 2 * p + 2, *from_minus)
        start_edges((1, 0), 2 * p, 2 * p + 2, *from_plus)

    for kind in range(2):
        for way in range(2):
            early(kind, way).wait_send()
            for p in range(2):
                late(kind, way, p).wait_send()

    def drain(j, carry):
        for kind in range(2):
            for way in range(2):
                fwd_copy(kind, way, j).wait_send()
        return carry

    lax.fori_loop(0, HALF, drain, 0)
    for side in range(2):

        @pl.when(has[side])
        def _(side=side):
            def body(j, carry):
                for kind in range(2):
                    edge_copy(kind, side, j).wait_send()
                return carry

            lax.fori_loop(0, BLK, body, 0)

        @pl.when(has[1 - side])
        def _(side=side):
            def body(j, carry):
                for kind in range(2):
                    edge_copy(kind, side, j).wait_recv()
                return carry

            lax.fori_loop(0, BLK, body, 0)


def near_kernel(lists_ref, counts_ref, win_t, win_q, out_ref, flat_g, flat_c, acc, outs, sem_o):
    start = lax.axis_index("leaf") * 32 - BLK
    mine = BLK + lax.axis_index("sub") * BLK

    def flatten(g, total):
        def one(s, carry):
            flat_g[total + s] = g
            flat_c[total + s] = lists_ref[g, s] - start
            return carry

        count = counts_ref[g]
        lax.fori_loop(0, count, one, 0)
        return total + count

    total = lax.fori_loop(0, BLK, flatten, 0)
    for i in range(PAIRS - 1):
        flat_g[total + i] = BLK
        flat_c[total + i] = mine
    acc[...] = jnp.zeros_like(acc)

    def step(i, carry):
        for k in range(PAIRS):
            g = flat_g[i * PAIRS + k]
            c = flat_c[i * PAIRS + k]
            target = win_t[mine + jnp.minimum(g, BLK - 1)]
            source = win_t[c]
            left = jnp.concatenate([target, tail_rows(half_squares(target.astype(F32)), 0, 3)], axis=0)
            right = jnp.concatenate([source, tail_rows(half_squares(source.astype(F32)), 3, 0)], axis=0)
            weights = jnp.exp2(dot_tn(left, right) * SCALE).astype(BF16)
            acc[g] += dot(weights, win_q[c])
        return carry

    lax.fori_loop(0, (total + PAIRS - 1) // PAIRS, step, 0)
    for g in range(BLK):
        outs[g] = acc[g] * (LEAF**-0.5)
        pltpu.make_async_copy(outs.at[g], out_ref.at[g], sem_o.at[g]).start()
    for g in range(BLK):
        pltpu.make_async_copy(outs.at[g], out_ref.at[g], sem_o.at[g]).wait()


def in_hbm(x):
    return pltpu.with_memory_space_constraint(x, pltpu.HBM)


def on_device(points, probes, order, near_lists, near_counts, leaf_sets, merge_sets):
    leaf_count = lax.axis_size("leaf")
    vmem = pl.BlockSpec(memory_space=pltpu.VMEM)
    hbm = pl.BlockSpec(memory_space=pltpu.HBM)
    smem = pl.BlockSpec(memory_space=pltpu.SMEM)
    window = 6 * BLK
    rounds = rounds_of(leaf_count)
    row_count = 7 + sum(n - 1 for _, _, n in rounds)
    dma = pltpu.SemaphoreType.DMA
    win_t, win_q, root = pl.pallas_call(
        functools.partial(gather_kernel, leaf_count),
        out_shape=(
            jax.ShapeDtypeStruct((window, DIM, LEAF), BF16),
            jax.ShapeDtypeStruct((window, LEAF, LANES), BF16),
            jax.ShapeDtypeStruct((8, LANES), F32),
        ),
        in_specs=[hbm] * 5,
        out_specs=(vmem, vmem, vmem),
        scratch_shapes=[
            pltpu.VMEM((DIM, BLK * LEAF), BF16),
            pltpu.VMEM((BLK * LEAF // LANES, LANES), jnp.int32),
            pltpu.VMEM((BLK, SKEL), jnp.int32),
            pltpu.VMEM((row_count, SKEL), jnp.int32),
            pltpu.VMEM((BLK, FORM - DIM, LEAF), BF16),
            pltpu.VMEM((BLK, NODE, LANES), BF16),
            pltpu.VMEM((len(rounds), 4, NODE, LANES), BF16),
            pltpu.VMEM((SKEL, LANES), F32),
            dma((4,)),
            dma((row_count,)),
            dma((2, 2)),
            dma((2, 2)),
            dma((2, 2, 2)),
            dma((2, 2, 2)),
            dma((2, 2, HALF)),
            dma((2, 2, HALF)),
            dma((2, 2, BLK)),
            dma((2, 2, BLK)),
            dma((len(rounds), 3)),
            dma((len(rounds), 3)),
        ],
        compiler_params=pltpu.CompilerParams(
            collective_id=0, has_side_effects=True, vmem_limit_bytes=32 * 2**20
        ),
        name="gather_and_tree",
    )(*map(in_hbm, (points.T, probes.reshape(BLK, LEAF, LANES), order.reshape(-1, LANES), leaf_sets, merge_sets)))
    near = pl.pallas_call(
        near_kernel,
        out_shape=jax.ShapeDtypeStruct((BLK, LEAF, LANES), F32),
        in_specs=[smem, smem, vmem, vmem],
        out_specs=hbm,
        scratch_shapes=[
            pltpu.SMEM((128,), jnp.int32),
            pltpu.SMEM((128,), jnp.int32),
            pltpu.VMEM((BLK + 1, LEAF, LANES), F32),
            pltpu.VMEM((BLK, LEAF, LANES), F32),
            dma((BLK,)),
        ],
        compiler_params=pltpu.CompilerParams(vmem_limit_bytes=32 * 2**20),
        name="near_field",
    )(in_hbm(near_lists), in_hbm(near_counts), win_t, win_q)
    return near.reshape(BLK * LEAF, LANES), root[0, :DIM]


def solution(mesh):
    both = P(("leaf", "sub"), None)
    in_specs = (both, both, P(("leaf", "sub")), both, P(("leaf", "sub")), both, P())
    out_specs = (both, P(("leaf", "sub")))
    return jax.shard_map(on_device, mesh=mesh, in_specs=in_specs, out_specs=out_specs, check_vma=False)
```

```python
import functools

import jax
import jax.numpy as jnp
from jax import lax
from jax.experimental import pallas as pl
from jax.experimental.pallas import tpu as pltpu
from jax.sharding import PartitionSpec as P

MESH = pl.DeviceIdType.MESH
BF16 = jnp.bfloat16
F32 = jnp.float32
LANES = 128
LEAF = 512
DIM = 64
FORM = DIM + 16
BLK = 8
HALF = 4
SKEL = 128
NODE = FORM + 2 * SKEL
PAIRS = 4
EARLY_STEPS = 2
FWD_STEPS = 1
LOG2E = 1.4426950408889634
SCALE = 2.0 * LOG2E / DIM


def dot(a, b):
    return jnp.dot(a, b, preferred_element_type=F32)


def dot_tn(a, b):
    return lax.dot_general(a, b, (((0,), (0,)), ((), ())), preferred_element_type=F32)


def half_squares(coords):
    h = -0.5 * jnp.sum(coords * coords, axis=0, keepdims=True)
    h1 = h.astype(BF16).astype(F32)
    h2 = (h - h1).astype(BF16).astype(F32)
    h3 = (h - h1 - h2).astype(BF16).astype(F32)
    return h1, h2, h3


def tail_rows(squares, first, ones):
    shape = (FORM - DIM, squares[0].shape[1])
    row = lax.broadcasted_iota(jnp.int32, shape, 0)
    tail = jnp.zeros(shape, F32)
    if ones is not None:
        tail = jnp.where((row >= ones) & (row < ones + 3), 1.0, tail)
    for i, part in enumerate(squares):
        tail = jnp.where(row == first + i, part, tail)
    return tail.astype(BF16)


def one_hot(row, height):
    shape = (height, row.shape[1])
    return jnp.where(lax.broadcasted_iota(jnp.int32, shape, 0) == row, 1.0, 0.0).astype(BF16)


def weigh(picked, coords):
    row = lax.broadcasted_iota(jnp.int32, picked.shape, 0)
    left = jnp.where((row >= DIM) & (row < DIM + 3), 1.0, picked).astype(BF16)
    return jnp.exp2(dot_tn(left, coords) * SCALE)


def hi_lo(x):
    hi = x.astype(BF16)
    return hi, (x - hi.astype(F32)).astype(BF16)


def node_of(picked, samples):
    return jnp.concatenate([picked.astype(BF16), *hi_lo(samples)], axis=0)


def merge(left, right, chosen):
    coords = jnp.concatenate([left[:FORM], right[:FORM]], axis=1)
    high = jnp.concatenate([left[FORM : FORM + SKEL], right[FORM : FORM + SKEL]], axis=0)
    low = jnp.concatenate([left[FORM + SKEL :], right[FORM + SKEL :]], axis=0)
    both = jnp.concatenate([high, low], axis=1)
    hot = one_hot(chosen, 2 * SKEL)
    picked = dot(coords, hot)
    kept = dot_tn(hot, both)
    weights = weigh(picked, coords)
    totals = jnp.sum(weights, axis=1, keepdims=True)
    w_hi, w_lo = hi_lo(weights)
    mixed = dot(w_hi, both)
    mixed = mixed[:, :LANES] + mixed[:, LANES:] + dot(w_lo, high)
    samples = kept[:, :LANES] + kept[:, LANES:] + mixed / totals
    return picked, samples


def rounds_of(leaf_count):
    rounds = [("sub", 1, 4), ("leaf", 1, 2)]
    d = 2
    while d < leaf_count:
        rounds.append(("leaf", d, 4 if 4 * d <= leaf_count else 2))
        d *= rounds[-1][2]
    return rounds


def pair_sum(target, source, probe):
    left = jnp.concatenate([target, tail_rows(half_squares(target.astype(F32)), 0, 3)], axis=0)
    right = jnp.concatenate([source, tail_rows(half_squares(source.astype(F32)), 3, 0)], axis=0)
    return dot(jnp.exp2(dot_tn(left, right) * SCALE).astype(BF16), probe)


def classify(block, shard_first, y):
    at = block - shard_first
    inside = (at >= 0) & (at < 4 * BLK)
    j = at & (BLK - 1)
    off = (lax.shift_right_arithmetic(at, 3) - y) & 3
    early = inside & ((off == 0) | ((off == 3) & (j < HALF)) | ((off == 1) & (j >= HALF)))
    return early, j + jnp.where(off == 0, 0, BLK), inside & (off == 2), j


def gather_kernel(
    leaf_count,
    lists,
    counts,
    points_hbm,
    probes_hbm,
    order_hbm,
    sets_hbm,
    merge_hbm,
    win_t,
    win_q,
    acc,
    root_ref,
    points,
    order,
    sets,
    chosen_rows,
    own_h,
    nodes,
    tree,
    final,
    early_t,
    early_q,
    fwd_t,
    fwd_q,
    plan,
    in_sem,
    row_sem,
    keep_sem,
    own_send,
    own_recv,
    late_send,
    late_recv,
    fwd_send,
    fwd_recv,
    edge_send,
    edge_recv,
    tree_send,
    tree_recv,
):
    leaf = lax.axis_index("leaf")
    y = lax.axis_index("sub")
    rank = leaf * 4 + y
    first_block = rank * BLK
    y_minus = lax.rem(y + 3, 4)
    y_plus = lax.rem(y + 1, 4)
    y_far = lax.rem(y + 2, 4)
    mine = BLK + y * BLK
    plus = (leaf, y_plus)
    minus = (leaf, y_minus)
    up = (lax.rem(leaf + 1, leaf_count), y)
    down = (lax.rem(leaf + leaf_count - 1, leaf_count), y)
    rounds = rounds_of(leaf_count)

    def partner(axis, d, n, k):
        place = y if axis == "sub" else leaf
        me = lax.rem(place // d, n)
        there = place + (lax.rem(me + k, n) - me) * d
        return me, ((leaf, there) if axis == "sub" else (there, y))

    inputs = [
        pltpu.make_async_copy(order_hbm, order, in_sem.at[0]),
        pltpu.make_async_copy(points_hbm, points, in_sem.at[1]),
        pltpu.make_async_copy(sets_hbm, sets, in_sem.at[2]),
        pltpu.make_async_copy(probes_hbm, early_q.at[pl.ds(0, BLK)], in_sem.at[3]),
    ]
    wanted = [first_block + i for i in range(7)]
    row_at = []
    for axis, d, n in rounds:
        span = BLK * d if axis == "sub" else BLK * 4 * d
        first = first_block // (n * span) * (n * span)
        row_at.append(len(wanted))
        wanted += [first + span - 1] if n == 2 else [first + span - 1, first + 3 * span - 1, first + 2 * span - 1]
    rows = [
        pltpu.make_async_copy(merge_hbm.at[pl.ds(w, 1)], chosen_rows.at[pl.ds(i, 1)], row_sem.at[i])
        for i, w in enumerate(wanted)
    ]
    for copy in inputs + rows:
        copy.start()

    greet = [up, down]
    for axis, d, n in rounds:
        if axis == "sub" or d > 1:
            greet += [partner(axis, d, n, k)[1] for k in range(1, n)]
    barrier = pltpu.get_barrier_semaphore()
    for who in greet:
        pl.semaphore_signal(barrier, inc=1, device_id=who, device_id_type=MESH)
    pl.semaphore_wait(barrier, len(greet))

    wins = (win_t, win_q)
    earlies = (early_t, early_q)
    fwds = (fwd_t, fwd_q)

    def remote(src, dst, send, recv, who):
        return pltpu.make_async_remote_copy(
            src_ref=src, dst_ref=dst, send_sem=send, recv_sem=recv, device_id=who, device_id_type=MESH
        )

    def own(kind, at, size):
        return (probes_hbm if kind else early_t).at[pl.ds(at, size)]

    def early(kind, way):
        return remote(
            own(kind, way * HALF, HALF),
            earlies[kind].at[pl.ds(BLK + way * HALF, HALF)],
            own_send.at[kind, way],
            own_recv.at[kind, way],
            minus if way else plus,
        )

    def late(kind, way, j):
        at = (1 - way) * HALF + j
        return remote(
            own(kind, at, 1),
            wins[kind].at[pl.ds(mine + at, 1)],
            late_send.at[kind, way, j],
            late_recv.at[kind, way, j],
            minus if way else plus,
        )

    def forward(kind, way, j):
        at = way * HALF + j
        return remote(
            earlies[kind].at[pl.ds(BLK + at, 1)],
            fwds[kind].at[pl.ds(at, 1)],
            fwd_send.at[kind, way, j],
            fwd_recv.at[kind, way, j],
            minus if way else plus,
        )

    def edge_copy(kind, side, j, source):
        if source == "own":
            src = own(kind, j, 1)
        elif source == "early":
            src = earlies[kind].at[pl.ds(BLK + j, 1)]
        elif source == "far":
            src = fwds[kind].at[pl.ds(j, 1)]
        else:
            src = wins[kind].at[pl.ds(BLK + (3 * BLK if side == 0 else 0) + j, 1)]
        return remote(
            src,
            wins[kind].at[pl.ds((0 if side == 0 else 5 * BLK) + j, 1)],
            edge_send.at[kind, side, j],
            edge_recv.at[kind, side, j],
            up if side == 0 else down,
        )

    has = (leaf < leaf_count - 1, leaf > 0)

    def start_edges(kinds, blocks, prev_when, next_when, source):
        for side, cond in ((0, prev_when), (1, next_when)):

            @pl.when(cond & has[side])
            def _(side=side):
                def body(j, carry):
                    for kind in kinds:
                        edge_copy(kind, side, j, source).start()
                    return carry

                lax.fori_loop(*blocks, body, 0)

    for way in range(2):
        early(1, way).start()
    start_edges((1,), (0, BLK), y == 3, y == 0, "own")

    inputs[0].wait()
    inputs[1].wait()

    def permute(i, carry):
        for k in range(2):
            b = 2 * i + k
            to = jnp.concatenate([order[pl.ds(b * 4 + q, 1), :] for q in range(4)], axis=1)
            at = pl.ds(pl.multiple_of(b * LEAF, LEAF), LEAF)
            coords = dot(points[:, at], one_hot(to, LEAF))
            early_t[b] = coords.astype(BF16)
            own_h[b] = tail_rows(half_squares(coords), 0, None)
        return carry

    lax.fori_loop(0, BLK // 2, permute, 0)
    for way in range(2):
        early(0, way).start()
    start_edges((0,), (0, BLK), y == 3, y == 0, "own")

    inputs[2].wait()
    inputs[3].wait()

    def leaf_nodes(i, carry):
        for k in range(4):
            b = 4 * i + k
            coords = jnp.concatenate([early_t[b], own_h[b]], axis=0)
            probe = early_q[b]
            hot = one_hot(sets[pl.ds(b, 1), :], LEAF)
            picked = dot(coords, hot)
            kept = dot_tn(hot, probe)
            weights = weigh(picked, coords)
            totals = jnp.sum(weights, axis=1, keepdims=True)
            w_hi, w_lo = hi_lo(weights)
            samples = kept + (dot(w_hi, probe) + dot(w_lo, probe)) / totals
            nodes[b] = node_of(picked, samples)
        return carry

    lax.fori_loop(0, BLK // 4, leaf_nodes, 0)
    for copy in rows:
        copy.wait()

    def row(i):
        return chosen_rows[i : i + 1, :]

    def merge_all(count, first, step):
        out = [node_of(*merge(nodes[2 * k], nodes[2 * k + 1], row(first + step * k))) for k in range(count)]
        for k in range(count):
            nodes[k] = out[k]

    merge_all(4, 0, 2)
    merge_all(2, 1, 4)
    state = merge(nodes[0], nodes[1], row(3))

    def plan_block(g, carry):
        count = counts[g]
        picks = [[g, 0] for _ in range(EARLY_STEPS)] + [[0, 0] for _ in range(FWD_STEPS)]
        seen_e = 0
        seen_f = 0
        for s in range(1, lists.shape[1]):
            is_e, at_e, is_f, at_f = classify(lists[g, s], leaf * 4 * BLK, y)
            is_e = is_e & (s < count)
            is_f = is_f & (s < count)
            for i in range(EARLY_STEPS):
                hit = is_e & (seen_e == i)
                picks[i] = [jnp.where(hit, at_e, picks[i][0]), jnp.where(hit, 1, picks[i][1])]
            for i in range(FWD_STEPS):
                hit = is_f & (seen_f == i)
                k = EARLY_STEPS + i
                picks[k] = [jnp.where(hit, at_f, picks[k][0]), jnp.where(hit, 1, picks[k][1])]
            seen_e = seen_e + is_e.astype(jnp.int32)
            seen_f = seen_f + is_f.astype(jnp.int32)
        for k, (at, on) in enumerate(picks):
            plan[g, 2 * k] = at
            plan[g, 2 * k + 1] = on
        return carry

    def self_pairs(i, carry):
        for k in range(4):
            g = 4 * i + k
            acc[g] = pair_sum(early_t[g], early_t[g], early_q[g])
        return carry

    def masked(g, k, t_ref, q_ref):
        at = plan[g, 2 * k]
        on = jnp.where(plan[g, 2 * k + 1] == 1, 1.0, 0.0)
        return pair_sum(early_t[g], t_ref[at], q_ref[at]) * on

    def early_pairs(i, carry):
        for g in (2 * i, 2 * i + 1):
            acc[g] += sum(masked(g, k, early_t, early_q) for k in range(EARLY_STEPS))
        return carry

    def fwd_pairs(i, carry):
        for h in range(4):
            g = 4 * i + h
            acc[g] += sum(masked(g, EARLY_STEPS + k, fwd_t, fwd_q) for k in range(FWD_STEPS))
        return carry

    def begin(i, state):
        axis, d, n = rounds[i]
        me, _ = partner(axis, d, n, 1)
        ref = tree.at[i, me]
        tree[i, me] = node_of(*state)
        copies = [
            remote(ref, ref, tree_send.at[i, k - 1], tree_recv.at[i, k - 1], partner(axis, d, n, k)[1])
            for k in range(1, n)
        ]
        for copy in copies:
            copy.start()
        return copies

    def finish(i, copies):
        for copy in copies:
            copy.wait()
        at = row_at[i]
        if rounds[i][2] == 2:
            return merge(tree[i, 0], tree[i, 1], row(at))
        low = node_of(*merge(tree[i, 0], tree[i, 1], row(at)))
        high = node_of(*merge(tree[i, 2], tree[i, 3], row(at + 1)))
        return merge(low, high, row(at + 2))

    from_minus = (y == 0, y == 1)
    from_plus = (y == 2, y == 3)

    copies = begin(0, state)
    for j in range(2):
        for way in range(2):
            late(1, way, j).start()
    lax.fori_loop(0, BLK, plan_block, 0)
    for kind in (1, 0):
        for way in range(2):
            early(kind, way).wait_recv()

    def send_on(j, carry):
        for way in range(2):
            for kind in (1, 0):
                forward(kind, way, j).start()
        return carry

    lax.fori_loop(0, HALF, send_on, 0)
    start_edges((1, 0), (0, HALF), *from_minus, "early")
    start_edges((1, 0), (HALF, BLK), *from_plus, "early")
    for j in range(HALF):
        for way in range(2):
            for kind in (1, 0):
                if not (kind == 1 and j < 2):
                    late(kind, way, j).start()
    keep = []
    for kind in range(2):
        for k, (at, size, there) in enumerate(
            (
                (0, BLK, mine),
                (BLK, HALF, BLK + y_minus * BLK),
                (BLK + HALF, HALF, BLK + y_plus * BLK + HALF),
            )
        ):
            keep.append(
                pltpu.make_async_copy(
                    earlies[kind].at[pl.ds(at, size)], wins[kind].at[pl.ds(there, size)], keep_sem.at[kind, k]
                )
            )
    for copy in keep:
        copy.start()
    state = finish(0, copies)

    def far(j, carry):
        for way in range(2):
            for kind in (1, 0):
                forward(kind, way, j).wait_recv()
        for side, cond in ((0, y == 1), (1, y == 2)):

            @pl.when(cond & has[side])
            def _(side=side):
                for way in range(2):
                    for kind in (1, 0):
                        edge_copy(kind, side, way * HALF + j, "far").start()

        return carry

    last = len(rounds) - 1
    fill = {1: (0, 1), last - 1: (3, 4)} if last > 2 else {}
    if last > 2:
        fill[2] = (1, 3)
    else:
        fill = {1: (0, 4)}
    for i in range(1, len(rounds)):
        copies = begin(i, state)
        if i == 1:
            lax.fori_loop(0, 2, self_pairs, 0)
        if i in fill:
            lax.fori_loop(*fill[i], early_pairs, 0)
        if i == last - 1:
            lax.fori_loop(0, HALF // 2, far, 0)
        if i == last:
            lax.fori_loop(HALF // 2, HALF, far, 0)
        state = finish(i, copies)
    for kind in range(2):
        copy = pltpu.make_async_copy(fwds[kind], wins[kind].at[pl.ds(BLK + y_far * BLK, BLK)], keep_sem.at[kind, 3])
        copy.start()
        keep.append(copy)
    final[...] = state[1]
    line = final[pl.ds(rank // 2 if leaf_count == 64 else 0, 1), :]
    line = jnp.broadcast_to(line, (8, LANES))
    root_ref[...] = jnp.where(lax.rem(rank, 2) == 1, pltpu.roll(line, DIM, 1), line)

    def second(j, carry):
        for way in range(2):
            for kind in (1, 0):
                late(kind, way, j).wait_recv()
        start_edges((1, 0), (HALF + j, HALF + j + 1), *from_minus, "late")
        start_edges((1, 0), (j, j + 1), *from_plus, "late")
        return carry

    lax.fori_loop(0, 2, second, 0)
    lax.fori_loop(0, 2, fwd_pairs, 0)
    lax.fori_loop(2, HALF, second, 0)

    for kind in range(2):
        for way in range(2):
            early(kind, way).wait_send()

    def drain(j, carry):
        for kind in range(2):
            for way in range(2):
                forward(kind, way, j).wait_send()
                late(kind, way, j).wait_send()
        return carry

    lax.fori_loop(0, HALF, drain, 0)
    for side in range(2):

        @pl.when(has[side])
        def _(side=side):
            def body(j, carry):
                for kind in range(2):
                    edge_copy(kind, side, j, "late").wait_send()
                return carry

            lax.fori_loop(0, BLK, body, 0)

        @pl.when(has[1 - side])
        def _(side=side):
            def body(j, carry):
                for kind in range(2):
                    edge_copy(kind, side, j, "late").wait_recv()
                return carry

            lax.fori_loop(0, BLK, body, 0)

    for copy in keep:
        copy.wait()


def near_kernel(lists, counts, win_t, win_q, part_ref, out_ref, flat_g, flat_c, acc, outs, sem_o):
    leaf = lax.axis_index("leaf")
    y = lax.axis_index("sub")
    mine = BLK + y * BLK

    def flatten(g, total):
        def one(s, carry):
            total, seen_e, seen_f = carry
            block = lists[g, s]
            is_e, _, is_f, _ = classify(block, leaf * 4 * BLK, y)
            done = (is_e & (seen_e < EARLY_STEPS)) | (is_f & (seen_f < FWD_STEPS))
            flat_g[total] = g
            flat_c[total] = block - (leaf * 4 * BLK - BLK)
            return (
                total + jnp.where(done, 0, 1),
                seen_e + is_e.astype(jnp.int32),
                seen_f + is_f.astype(jnp.int32),
            )

        return lax.fori_loop(1, counts[g], one, (total, jnp.int32(0), jnp.int32(0)))[0]

    total = lax.fori_loop(0, BLK, flatten, jnp.int32(0))
    for i in range(PAIRS - 1):
        flat_g[total + i] = BLK
        flat_c[total + i] = mine
    acc[:BLK] = part_ref[...]
    acc[BLK] = jnp.zeros((LEAF, LANES), F32)

    def step(i, carry):
        for k in range(PAIRS):
            g = flat_g[i * PAIRS + k]
            c = flat_c[i * PAIRS + k]
            acc[g] += pair_sum(win_t[mine + jnp.minimum(g, BLK - 1)], win_t[c], win_q[c])
        return carry

    lax.fori_loop(0, (total + PAIRS - 1) // PAIRS, step, 0)
    for g in range(BLK):
        outs[g] = acc[g] * (LEAF**-0.5)
        pltpu.make_async_copy(outs.at[g], out_ref.at[g], sem_o.at[g]).start()
    for g in range(BLK):
        pltpu.make_async_copy(outs.at[g], out_ref.at[g], sem_o.at[g]).wait()


def in_hbm(x):
    return pltpu.with_memory_space_constraint(x, pltpu.HBM)


def on_device(points, probes, order, near_lists, near_counts, leaf_sets, merge_sets):
    leaf_count = lax.axis_size("leaf")
    vmem = pl.BlockSpec(memory_space=pltpu.VMEM)
    hbm = pl.BlockSpec(memory_space=pltpu.HBM)
    smem = pl.BlockSpec(memory_space=pltpu.SMEM)
    window = 6 * BLK
    rounds = rounds_of(leaf_count)
    row_count = 7 + sum(n - 1 for _, _, n in rounds)
    dma = pltpu.SemaphoreType.DMA
    win_t, win_q, part, root = pl.pallas_call(
        functools.partial(gather_kernel, leaf_count),
        out_shape=(
            jax.ShapeDtypeStruct((window, DIM, LEAF), BF16),
            jax.ShapeDtypeStruct((window, LEAF, LANES), BF16),
            jax.ShapeDtypeStruct((BLK, LEAF, LANES), F32),
            jax.ShapeDtypeStruct((8, LANES), F32),
        ),
        in_specs=[smem, smem] + [hbm] * 5,
        out_specs=(vmem,) * 4,
        scratch_shapes=[
            pltpu.VMEM((DIM, BLK * LEAF), BF16),
            pltpu.VMEM((BLK * LEAF // LANES, LANES), jnp.int32),
            pltpu.VMEM((BLK, SKEL), jnp.int32),
            pltpu.VMEM((row_count, SKEL), jnp.int32),
            pltpu.VMEM((BLK, FORM - DIM, LEAF), BF16),
            pltpu.VMEM((BLK, NODE, LANES), BF16),
            pltpu.VMEM((len(rounds), 4, NODE, LANES), BF16),
            pltpu.VMEM((SKEL, LANES), F32),
            pltpu.VMEM((2 * BLK, DIM, LEAF), BF16),
            pltpu.VMEM((2 * BLK, LEAF, LANES), BF16),
            pltpu.VMEM((BLK, DIM, LEAF), BF16),
            pltpu.VMEM((BLK, LEAF, LANES), BF16),
            pltpu.SMEM((BLK, 2 * (EARLY_STEPS + FWD_STEPS)), jnp.int32),
            dma((4,)),
            dma((row_count,)),
            dma((2, 4)),
            dma((2, 2)),
            dma((2, 2)),
            dma((2, 2, HALF)),
            dma((2, 2, HALF)),
            dma((2, 2, HALF)),
            dma((2, 2, HALF)),
            dma((2, 2, BLK)),
            dma((2, 2, BLK)),
            dma((len(rounds), 3)),
            dma((len(rounds), 3)),
        ],
        compiler_params=pltpu.CompilerParams(
            collective_id=0, has_side_effects=True, vmem_limit_bytes=32 * 2**20
        ),
        name="gather_and_tree",
    )(*map(in_hbm, (near_lists, near_counts, points.T, probes.reshape(BLK, LEAF, LANES), order.reshape(-1, LANES), leaf_sets, merge_sets)))
    near = pl.pallas_call(
        near_kernel,
        out_shape=jax.ShapeDtypeStruct((BLK, LEAF, LANES), F32),
        in_specs=[smem, smem, vmem, vmem, vmem],
        out_specs=hbm,
        scratch_shapes=[
            pltpu.SMEM((128,), jnp.int32),
            pltpu.SMEM((128,), jnp.int32),
            pltpu.VMEM((BLK + 1, LEAF, LANES), F32),
            pltpu.VMEM((BLK, LEAF, LANES), F32),
            dma((BLK,)),
        ],
        compiler_params=pltpu.CompilerParams(vmem_limit_bytes=32 * 2**20),
        name="near_field",
    )(in_hbm(near_lists), in_hbm(near_counts), win_t, win_q, part)
    return near.reshape(BLK * LEAF, LANES), root[0, :DIM]


def solution(mesh):
    both = P(("leaf", "sub"), None)
    in_specs = (both, both, P(("leaf", "sub")), both, P(("leaf", "sub")), both, P())
    out_specs = (both, P(("leaf", "sub")))
    return jax.shard_map(on_device, mesh=mesh, in_specs=in_specs, out_specs=out_specs, check_vma=False)
```

```python
import functools

import jax
import jax.numpy as jnp
from jax import lax
from jax.experimental import pallas as pl
from jax.experimental.pallas import tpu as pltpu
from jax.sharding import PartitionSpec as P

MESH = pl.DeviceIdType.MESH
BF16 = jnp.bfloat16
F32 = jnp.float32
LANES = 128
LEAF = 512
DIM = 64
FORM = DIM + 16
BLK = 8
HALF = 4
SKEL = 128
NODE = FORM + 2 * SKEL
PAIRS = 4
STEPS = (2, 1, 1)
LOG2E = 1.4426950408889634
SCALE = 2.0 * LOG2E / DIM


def dot(a, b):
    return jnp.dot(a, b, preferred_element_type=F32)


def dot_tn(a, b):
    return lax.dot_general(a, b, (((0,), (0,)), ((), ())), preferred_element_type=F32)


def half_squares(coords):
    h = -0.5 * jnp.sum(coords * coords, axis=0, keepdims=True)
    h1 = h.astype(BF16).astype(F32)
    h2 = (h - h1).astype(BF16).astype(F32)
    h3 = (h - h1 - h2).astype(BF16).astype(F32)
    return h1, h2, h3


def tail_rows(squares, first, ones):
    shape = (FORM - DIM, squares[0].shape[1])
    row = lax.broadcasted_iota(jnp.int32, shape, 0)
    tail = jnp.zeros(shape, F32)
    if ones is not None:
        tail = jnp.where((row >= ones) & (row < ones + 3), 1.0, tail)
    for i, part in enumerate(squares):
        tail = jnp.where(row == first + i, part, tail)
    return tail.astype(BF16)


def one_hot(row, height):
    shape = (height, row.shape[1])
    return jnp.where(lax.broadcasted_iota(jnp.int32, shape, 0) == row, 1.0, 0.0).astype(BF16)


def weigh(picked, coords):
    row = lax.broadcasted_iota(jnp.int32, picked.shape, 0)
    left = jnp.where((row >= DIM) & (row < DIM + 3), 1.0, picked).astype(BF16)
    return jnp.exp2(dot_tn(left, coords) * SCALE)


def hi_lo(x):
    hi = x.astype(BF16)
    return hi, (x - hi.astype(F32)).astype(BF16)


def node_of(picked, samples):
    return jnp.concatenate([picked.astype(BF16), *hi_lo(samples)], axis=0)


def merge(left, right, chosen):
    coords = jnp.concatenate([left[:FORM], right[:FORM]], axis=1)
    high = jnp.concatenate([left[FORM : FORM + SKEL], right[FORM : FORM + SKEL]], axis=0)
    low = jnp.concatenate([left[FORM + SKEL :], right[FORM + SKEL :]], axis=0)
    both = jnp.concatenate([high, low], axis=1)
    hot = one_hot(chosen, 2 * SKEL)
    picked = dot(coords, hot)
    kept = dot_tn(hot, both)
    weights = weigh(picked, coords)
    totals = jnp.sum(weights, axis=1, keepdims=True)
    w_hi, w_lo = hi_lo(weights)
    mixed = dot(w_hi, both)
    mixed = mixed[:, :LANES] + mixed[:, LANES:] + dot(w_lo, high)
    samples = kept[:, :LANES] + kept[:, LANES:] + mixed / totals
    return picked, samples


def rounds_of(leaf_count):
    rounds = [("sub", 1, 4), ("leaf", 1, 2)]
    d = 2
    while d < leaf_count:
        rounds.append(("leaf", d, 4 if 4 * d <= leaf_count else 2))
        d *= rounds[-1][2]
    return rounds


def pair_sum(target, source, probe):
    left = jnp.concatenate([target, tail_rows(half_squares(target.astype(F32)), 0, 3)], axis=0)
    right = jnp.concatenate([source, tail_rows(half_squares(source.astype(F32)), 3, 0)], axis=0)
    return dot(jnp.exp2(dot_tn(left, right) * SCALE).astype(BF16), probe)


def classify(block, shard_first, y):
    at = block - shard_first
    inside = (at >= 0) & (at < 4 * BLK)
    j = at & (BLK - 1)
    off = (lax.shift_right_arithmetic(at, 3) - y) & 3
    early = inside & ((off == 0) | ((off == 3) & (j < HALF)) | ((off == 1) & (j >= HALF)))
    side = jnp.where(at < 0, 0, 1)
    last = (side == (y & 1)) & ((j < HALF) == (y >= 2))
    edge = jnp.logical_not(inside) & jnp.logical_not(last)
    return [(early, j + jnp.where(off == 0, 0, BLK)), (inside & (off == 2), j), (edge, side * BLK + j)]


def gather_kernel(
    leaf_count,
    lists,
    counts,
    points_hbm,
    probes_hbm,
    order_hbm,
    sets_hbm,
    merge_hbm,
    win_t,
    win_q,
    acc,
    root_ref,
    points,
    order,
    sets,
    chosen_rows,
    own_h,
    nodes,
    tree,
    final,
    early_t,
    early_q,
    fwd_t,
    fwd_q,
    edge_t,
    edge_q,
    plan,
    in_sem,
    row_sem,
    keep_sem,
    own_send,
    own_recv,
    late_send,
    late_recv,
    fwd_send,
    fwd_recv,
    edge_send,
    edge_recv,
    tree_send,
    tree_recv,
):
    leaf = lax.axis_index("leaf")
    y = lax.axis_index("sub")
    rank = leaf * 4 + y
    first_block = rank * BLK
    y_minus = lax.rem(y + 3, 4)
    y_plus = lax.rem(y + 1, 4)
    y_far = lax.rem(y + 2, 4)
    mine = BLK + y * BLK
    plus = (leaf, y_plus)
    minus = (leaf, y_minus)
    up = (lax.rem(leaf + 1, leaf_count), y)
    down = (lax.rem(leaf + leaf_count - 1, leaf_count), y)
    rounds = rounds_of(leaf_count)

    def partner(axis, d, n, k):
        place = y if axis == "sub" else leaf
        me = lax.rem(place // d, n)
        there = place + (lax.rem(me + k, n) - me) * d
        return me, ((leaf, there) if axis == "sub" else (there, y))

    inputs = [
        pltpu.make_async_copy(order_hbm, order, in_sem.at[0]),
        pltpu.make_async_copy(points_hbm, points, in_sem.at[1]),
        pltpu.make_async_copy(sets_hbm, sets, in_sem.at[2]),
        pltpu.make_async_copy(probes_hbm, early_q.at[pl.ds(0, BLK)], in_sem.at[3]),
    ]
    wanted = [first_block + i for i in range(7)]
    row_at = []
    for axis, d, n in rounds:
        span = BLK * d if axis == "sub" else BLK * 4 * d
        first = first_block // (n * span) * (n * span)
        row_at.append(len(wanted))
        wanted += [first + span - 1] if n == 2 else [first + span - 1, first + 3 * span - 1, first + 2 * span - 1]
    rows = [
        pltpu.make_async_copy(merge_hbm.at[pl.ds(w, 1)], chosen_rows.at[pl.ds(i, 1)], row_sem.at[i])
        for i, w in enumerate(wanted)
    ]
    for copy in inputs + rows:
        copy.start()

    greet = [up, down]
    for axis, d, n in rounds:
        if axis == "sub" or d > 1:
            greet += [partner(axis, d, n, k)[1] for k in range(1, n)]
    barrier = pltpu.get_barrier_semaphore()
    for who in greet:
        pl.semaphore_signal(barrier, inc=1, device_id=who, device_id_type=MESH)
    pl.semaphore_wait(barrier, len(greet))

    wins = (win_t, win_q)
    earlies = (early_t, early_q)
    fwds = (fwd_t, fwd_q)
    edges = (edge_t, edge_q)
    near_side = y & 1
    soon = (y // 2) * HALF

    def remote(src, dst, send, recv, who):
        return pltpu.make_async_remote_copy(
            src_ref=src, dst_ref=dst, send_sem=send, recv_sem=recv, device_id=who, device_id_type=MESH
        )

    def own(kind, at, size):
        return (probes_hbm if kind else early_t).at[pl.ds(at, size)]

    def early(kind, way):
        return remote(
            own(kind, way * HALF, HALF),
            earlies[kind].at[pl.ds(BLK + way * HALF, HALF)],
            own_send.at[kind, way],
            own_recv.at[kind, way],
            minus if way else plus,
        )

    def late(kind, way, j):
        at = (1 - way) * HALF + j
        return remote(
            own(kind, at, 1),
            wins[kind].at[pl.ds(mine + at, 1)],
            late_send.at[kind, way, j],
            late_recv.at[kind, way, j],
            minus if way else plus,
        )

    def forward(kind, way, j):
        at = way * HALF + j
        return remote(
            earlies[kind].at[pl.ds(BLK + at, 1)],
            fwds[kind].at[pl.ds(at, 1)],
            fwd_send.at[kind, way, j],
            fwd_recv.at[kind, way, j],
            minus if way else plus,
        )

    def edge_copy(kind, side, j, source):
        if source == "own":
            src = own(kind, j, 1)
        elif source == "early":
            src = earlies[kind].at[pl.ds(BLK + j, 1)]
        elif source == "far":
            src = fwds[kind].at[pl.ds(j, 1)]
        else:
            src = wins[kind].at[pl.ds(BLK + (3 * BLK if side == 0 else 0) + j, 1)]
        there = wins[kind].at[pl.ds((0 if side == 0 else 5 * BLK) + j, 1)]
        return remote(
            src,
            there if source == "late" else edges[kind].at[pl.ds(side * BLK + j, 1)],
            edge_send.at[kind, side, j],
            edge_recv.at[kind, side, j],
            up if side == 0 else down,
        )

    has = (leaf < leaf_count - 1, leaf > 0)

    def start_edges(kinds, blocks, prev_when, next_when, source):
        for side, cond in ((0, prev_when), (1, next_when)):

            @pl.when(cond & has[side])
            def _(side=side):
                def body(j, carry):
                    for kind in kinds:
                        edge_copy(kind, side, j, source).start()
                    return carry

                lax.fori_loop(*blocks, body, 0)

    for way in range(2):
        early(1, way).start()
    start_edges((1,), (0, BLK), y == 3, y == 0, "own")

    inputs[0].wait()
    inputs[1].wait()

    def permute(i, carry):
        for k in range(2):
            b = 2 * i + k
            to = jnp.concatenate([order[pl.ds(b * 4 + q, 1), :] for q in range(4)], axis=1)
            at = pl.ds(pl.multiple_of(b * LEAF, LEAF), LEAF)
            coords = dot(points[:, at], one_hot(to, LEAF))
            early_t[b] = coords.astype(BF16)
            own_h[b] = tail_rows(half_squares(coords), 0, None)
        return carry

    lax.fori_loop(0, BLK // 2, permute, 0)
    for way in range(2):
        early(0, way).start()
    start_edges((0,), (0, BLK), y == 3, y == 0, "own")

    inputs[2].wait()
    inputs[3].wait()

    def leaf_nodes(i, carry):
        for k in range(4):
            b = 4 * i + k
            coords = jnp.concatenate([early_t[b], own_h[b]], axis=0)
            probe = early_q[b]
            hot = one_hot(sets[pl.ds(b, 1), :], LEAF)
            picked = dot(coords, hot)
            kept = dot_tn(hot, probe)
            weights = weigh(picked, coords)
            totals = jnp.sum(weights, axis=1, keepdims=True)
            w_hi, w_lo = hi_lo(weights)
            samples = kept + (dot(w_hi, probe) + dot(w_lo, probe)) / totals
            nodes[b] = node_of(picked, samples)
        return carry

    lax.fori_loop(0, BLK // 4, leaf_nodes, 0)
    for copy in rows:
        copy.wait()

    def row(i):
        return chosen_rows[i : i + 1, :]

    def merge_all(count, first, step):
        out = [node_of(*merge(nodes[2 * k], nodes[2 * k + 1], row(first + step * k))) for k in range(count)]
        for k in range(count):
            nodes[k] = out[k]

    merge_all(4, 0, 2)
    merge_all(2, 1, 4)
    state = merge(nodes[0], nodes[1], row(3))

    stocks = ((early_t, early_q), (fwd_t, fwd_q), (edge_t, edge_q))
    spare = (0, 0, jnp.where(leaf > 0, 0, BLK) + soon)
    first_step = (0, STEPS[0], STEPS[0] + STEPS[1])

    def plan_block(g, carry):
        count = counts[g]
        picks = [[[spare[c], 0] for _ in range(STEPS[c])] for c in range(3)]
        seen = [0, 0, 0]
        for s in range(1, lists.shape[1]):
            for c, (there, at) in enumerate(classify(lists[g, s], leaf * 4 * BLK, y)):
                there = there & (s < count)
                for pick, i in zip(picks[c], range(STEPS[c])):
                    hit = there & (seen[c] == i)
                    pick[:] = jnp.where(hit, at, pick[0]), jnp.where(hit, 1, pick[1])
                seen[c] = seen[c] + there.astype(jnp.int32)
        for c in range(3):
            for i in range(STEPS[c]):
                plan[g, 2 * (first_step[c] + i)] = picks[c][i][0]
                plan[g, 2 * (first_step[c] + i) + 1] = picks[c][i][1]
        return carry

    def self_pairs(i, carry):
        for k in range(4):
            g = 4 * i + k
            acc[g] = pair_sum(early_t[g], early_t[g], early_q[g])
        return carry

    def pairs_from(c):
        width = 4 // STEPS[c]

        def body(i, carry):
            for h in range(width):
                g = width * i + h
                total = acc[g]
                for k in range(first_step[c], first_step[c] + STEPS[c]):
                    at = plan[g, 2 * k]
                    on = jnp.where(plan[g, 2 * k + 1] == 1, 1.0, 0.0)
                    total = total + pair_sum(early_t[g], stocks[c][0][at], stocks[c][1][at]) * on
                acc[g] = total
            return carry

        return body

    def begin(i, state):
        axis, d, n = rounds[i]
        me, _ = partner(axis, d, n, 1)
        ref = tree.at[i, me]
        tree[i, me] = node_of(*state)
        copies = [
            remote(ref, ref, tree_send.at[i, k - 1], tree_recv.at[i, k - 1], partner(axis, d, n, k)[1])
            for k in range(1, n)
        ]
        for copy in copies:
            copy.start()
        return copies

    def finish(i, copies):
        for copy in copies:
            copy.wait()
        at = row_at[i]
        if rounds[i][2] == 2:
            return merge(tree[i, 0], tree[i, 1], row(at))
        low = node_of(*merge(tree[i, 0], tree[i, 1], row(at)))
        high = node_of(*merge(tree[i, 2], tree[i, 3], row(at + 1)))
        return merge(low, high, row(at + 2))

    from_minus = (y == 0, y == 1)
    from_plus = (y == 2, y == 3)

    copies = begin(0, state)
    for way in range(2):
        late(1, way, 0).start()
    lax.fori_loop(0, BLK, plan_block, 0)
    lax.fori_loop(0, 2, self_pairs, 0)
    for kind in (1, 0):
        for way in range(2):
            early(kind, way).wait_recv()

    def send_on(j, carry):
        for way in range(2):
            for kind in (1, 0):
                forward(kind, way, j).start()
        return carry

    lax.fori_loop(0, HALF, send_on, 0)
    start_edges((1, 0), (0, HALF), *from_minus, "early")
    start_edges((1, 0), (HALF, BLK), *from_plus, "early")
    for j in range(HALF):
        for way in range(2):
            for kind in (1, 0):
                if not (kind == 1 and j == 0):
                    late(kind, way, j).start()
    keep = []
    for kind in range(2):
        for k, (at, size, there) in enumerate(
            (
                (0, BLK, mine),
                (BLK, HALF, BLK + y_minus * BLK),
                (BLK + HALF, HALF, BLK + y_plus * BLK + HALF),
            )
        ):
            keep.append(
                pltpu.make_async_copy(
                    earlies[kind].at[pl.ds(at, size)], wins[kind].at[pl.ds(there, size)], keep_sem.at[kind, k]
                )
            )
    for copy in keep:
        copy.start()
    state = finish(0, copies)

    def far(j, carry):
        for way in range(2):
            for kind in (1, 0):
                forward(kind, way, j).wait_recv()
        for side, cond in ((0, y == 1), (1, y == 2)):

            @pl.when(cond & has[side])
            def _(side=side):
                for way in range(2):
                    for kind in (1, 0):
                        edge_copy(kind, side, way * HALF + j, "far").start()

        return carry

    last = len(rounds) - 1
    e_step, f_step = pairs_from(0), pairs_from(1)
    if last == 4:
        fill = {
            2: ((e_step, 0, 1), (far, 0, 1), (e_step, 1, 2), (far, 1, 2)),
            3: ((e_step, 2, 3), (far, 2, 3), (e_step, 3, 4), (far, 3, 4)),
            4: ((f_step, 0, 2),),
        }
    else:
        fill = {last: ((e_step, 0, 4), (far, 0, 4), (f_step, 0, 2))}
    for i in range(1, len(rounds)):
        copies = begin(i, state)
        for what, start, end in fill.get(i, ()):
            lax.fori_loop(start, end, what, 0)
        state = finish(i, copies)
    for kind in range(2):
        copy = pltpu.make_async_copy(fwds[kind], wins[kind].at[pl.ds(BLK + y_far * BLK, BLK)], keep_sem.at[kind, 3])
        copy.start()
        keep.append(copy)
    final[...] = state[1]
    line = final[pl.ds(rank // 2 if leaf_count == 64 else 0, 1), :]
    line = jnp.broadcast_to(line, (8, LANES))
    root_ref[...] = jnp.where(lax.rem(rank, 2) == 1, pltpu.roll(line, DIM, 1), line)

    def second(j, carry):
        for way in range(2):
            for kind in (1, 0):
                late(kind, way, j).wait_recv()
        start_edges((1, 0), (HALF + j, HALF + j + 1), *from_minus, "late")
        start_edges((1, 0), (j, j + 1), *from_plus, "late")
        return carry

    def await_edges(near_from, others):
        for side in range(2):

            @pl.when(has[1 - side])
            def _(side=side):
                def body(j, carry):
                    for kind in range(2):
                        edge_copy(kind, side, j, "late" if not others else "far").wait_recv()
                    return carry

                @pl.when(near_side == side)
                def _():
                    lax.fori_loop(near_from, near_from + HALF, body, 0)

                if others:

                    @pl.when(near_side != side)
                    def _():
                        lax.fori_loop(0, BLK, body, 0)

    lax.fori_loop(0, HALF, second, 0)
    await_edges(soon, True)
    for kind in range(2):
        for k, (at, size, there) in enumerate(
            (
                (near_side * BLK + soon, HALF, near_side * 5 * BLK + soon),
                ((1 - near_side) * BLK, BLK, (1 - near_side) * 5 * BLK),
            )
        ):
            copy = pltpu.make_async_copy(
                edges[kind].at[pl.ds(at, size)], wins[kind].at[pl.ds(there, size)], keep_sem.at[kind, 4 + k]
            )
            copy.start()
            keep.append(copy)
    lax.fori_loop(0, BLK * STEPS[2] // 4, pairs_from(2), 0)

    for kind in range(2):
        for way in range(2):
            early(kind, way).wait_send()

    def drain(j, carry):
        for kind in range(2):
            for way in range(2):
                forward(kind, way, j).wait_send()
                late(kind, way, j).wait_send()
        return carry

    lax.fori_loop(0, HALF, drain, 0)
    for side in range(2):

        @pl.when(has[side])
        def _(side=side):
            def body(j, carry):
                for kind in range(2):
                    edge_copy(kind, side, j, "late").wait_send()
                return carry

            lax.fori_loop(0, BLK, body, 0)

    await_edges(HALF - soon, False)
    for copy in keep:
        copy.wait()


def near_kernel(lists, counts, win_t, win_q, part_ref, out_ref, flat_g, flat_c, acc, outs, sem_o):
    leaf = lax.axis_index("leaf")
    y = lax.axis_index("sub")
    mine = BLK + y * BLK

    def flatten(g, total):
        def one(s, carry):
            total, *seen = carry
            block = lists[g, s]
            done = False
            for c, (there, _) in enumerate(classify(block, leaf * 4 * BLK, y)):
                done = done | (there & (seen[c] < STEPS[c]))
                seen[c] = seen[c] + there.astype(jnp.int32)
            flat_g[total] = g
            flat_c[total] = block - (leaf * 4 * BLK - BLK)
            return (total + jnp.where(done, 0, 1), *seen)

        zero = jnp.int32(0)
        return lax.fori_loop(1, counts[g], one, (total, zero, zero, zero))[0]

    total = lax.fori_loop(0, BLK, flatten, jnp.int32(0))
    for i in range(PAIRS - 1):
        flat_g[total + i] = BLK
        flat_c[total + i] = mine
    acc[:BLK] = part_ref[...]
    acc[BLK] = jnp.zeros((LEAF, LANES), F32)

    def step(i, carry):
        for k in range(PAIRS):
            g = flat_g[i * PAIRS + k]
            c = flat_c[i * PAIRS + k]
            acc[g] += pair_sum(win_t[mine + jnp.minimum(g, BLK - 1)], win_t[c], win_q[c])
        return carry

    lax.fori_loop(0, (total + PAIRS - 1) // PAIRS, step, 0)
    for g in range(BLK):
        outs[g] = acc[g] * (LEAF**-0.5)
        pltpu.make_async_copy(outs.at[g], out_ref.at[g], sem_o.at[g]).start()
    for g in range(BLK):
        pltpu.make_async_copy(outs.at[g], out_ref.at[g], sem_o.at[g]).wait()


def in_hbm(x):
    return pltpu.with_memory_space_constraint(x, pltpu.HBM)


def on_device(points, probes, order, near_lists, near_counts, leaf_sets, merge_sets):
    leaf_count = lax.axis_size("leaf")
    vmem = pl.BlockSpec(memory_space=pltpu.VMEM)
    hbm = pl.BlockSpec(memory_space=pltpu.HBM)
    smem = pl.BlockSpec(memory_space=pltpu.SMEM)
    window = 6 * BLK
    rounds = rounds_of(leaf_count)
    row_count = 7 + sum(n - 1 for _, _, n in rounds)
    dma = pltpu.SemaphoreType.DMA
    win_t, win_q, part, root = pl.pallas_call(
        functools.partial(gather_kernel, leaf_count),
        out_shape=(
            jax.ShapeDtypeStruct((window, DIM, LEAF), BF16),
            jax.ShapeDtypeStruct((window, LEAF, LANES), BF16),
            jax.ShapeDtypeStruct((BLK, LEAF, LANES), F32),
            jax.ShapeDtypeStruct((8, LANES), F32),
        ),
        in_specs=[smem, smem] + [hbm] * 5,
        out_specs=(vmem,) * 4,
        scratch_shapes=[
            pltpu.VMEM((DIM, BLK * LEAF), BF16),
            pltpu.VMEM((BLK * LEAF // LANES, LANES), jnp.int32),
            pltpu.VMEM((BLK, SKEL), jnp.int32),
            pltpu.VMEM((row_count, SKEL), jnp.int32),
            pltpu.VMEM((BLK, FORM - DIM, LEAF), BF16),
            pltpu.VMEM((BLK, NODE, LANES), BF16),
            pltpu.VMEM((len(rounds), 4, NODE, LANES), BF16),
            pltpu.VMEM((SKEL, LANES), F32),
            pltpu.VMEM((2 * BLK, DIM, LEAF), BF16),
            pltpu.VMEM((2 * BLK, LEAF, LANES), BF16),
            pltpu.VMEM((BLK, DIM, LEAF), BF16),
            pltpu.VMEM((BLK, LEAF, LANES), BF16),
            pltpu.VMEM((2 * BLK, DIM, LEAF), BF16),
            pltpu.VMEM((2 * BLK, LEAF, LANES), BF16),
            pltpu.SMEM((BLK, 2 * sum(STEPS)), jnp.int32),
            dma((4,)),
            dma((row_count,)),
            dma((2, 6)),
            dma((2, 2)),
            dma((2, 2)),
            dma((2, 2, HALF)),
            dma((2, 2, HALF)),
            dma((2, 2, HALF)),
            dma((2, 2, HALF)),
            dma((2, 2, BLK)),
            dma((2, 2, BLK)),
            dma((len(rounds), 3)),
            dma((len(rounds), 3)),
        ],
        compiler_params=pltpu.CompilerParams(
            collective_id=0, has_side_effects=True, vmem_limit_bytes=32 * 2**20
        ),
        name="gather_and_tree",
    )(*map(in_hbm, (near_lists, near_counts, points.T, probes.reshape(BLK, LEAF, LANES), order.reshape(-1, LANES), leaf_sets, merge_sets)))
    near = pl.pallas_call(
        near_kernel,
        out_shape=jax.ShapeDtypeStruct((BLK, LEAF, LANES), F32),
        in_specs=[smem, smem, vmem, vmem, vmem],
        out_specs=hbm,
        scratch_shapes=[
            pltpu.SMEM((128,), jnp.int32),
            pltpu.SMEM((128,), jnp.int32),
            pltpu.VMEM((BLK + 1, LEAF, LANES), F32),
            pltpu.VMEM((BLK, LEAF, LANES), F32),
            dma((BLK,)),
        ],
        compiler_params=pltpu.CompilerParams(vmem_limit_bytes=32 * 2**20),
        name="near_field",
    )(in_hbm(near_lists), in_hbm(near_counts), win_t, win_q, part)
    return near.reshape(BLK * LEAF, LANES), root[0, :DIM]


def solution(mesh):
    both = P(("leaf", "sub"), None)
    in_specs = (both, both, P(("leaf", "sub")), both, P(("leaf", "sub")), both, P())
    out_specs = (both, P(("leaf", "sub")))
    return jax.shard_map(on_device, mesh=mesh, in_specs=in_specs, out_specs=out_specs, check_vma=False)
```

```python
import functools

import jax
import jax.numpy as jnp
from jax import lax
from jax.experimental import pallas as pl
from jax.experimental.pallas import tpu as pltpu
from jax.sharding import PartitionSpec as P

MESH = pl.DeviceIdType.MESH
BF16 = jnp.bfloat16
F32 = jnp.float32
LANES = 128
LEAF = 512
DIM = 64
FORM = DIM + 16
BLK = 8
HALF = 4
SKEL = 128
NODE = FORM + 2 * SKEL
PAIRS = 4
STEPS = (2, 2, 2, 1)
LOG2E = 1.4426950408889634
SCALE = 2.0 * LOG2E / DIM


def dot(a, b):
    return jnp.dot(a, b, preferred_element_type=F32)


def dot_tn(a, b):
    return lax.dot_general(a, b, (((0,), (0,)), ((), ())), preferred_element_type=F32)


def half_squares(coords):
    h = -0.5 * jnp.sum(coords * coords, axis=0, keepdims=True)
    h1 = h.astype(BF16).astype(F32)
    h2 = (h - h1).astype(BF16).astype(F32)
    h3 = (h - h1 - h2).astype(BF16).astype(F32)
    return h1, h2, h3


def tail_rows(squares, first, ones):
    shape = (FORM - DIM, squares[0].shape[1])
    row = lax.broadcasted_iota(jnp.int32, shape, 0)
    tail = jnp.zeros(shape, F32)
    if ones is not None:
        tail = jnp.where((row >= ones) & (row < ones + 3), 1.0, tail)
    for i, part in enumerate(squares):
        tail = jnp.where(row == first + i, part, tail)
    return tail.astype(BF16)


def one_hot(row, height):
    shape = (height, row.shape[1])
    return jnp.where(lax.broadcasted_iota(jnp.int32, shape, 0) == row, 1.0, 0.0).astype(BF16)


def weigh(picked, coords):
    row = lax.broadcasted_iota(jnp.int32, picked.shape, 0)
    left = jnp.where((row >= DIM) & (row < DIM + 3), 1.0, picked).astype(BF16)
    return jnp.exp2(dot_tn(left, coords) * SCALE)


def hi_lo(x):
    hi = x.astype(BF16)
    return hi, (x - hi.astype(F32)).astype(BF16)


def node_of(picked, samples):
    return jnp.concatenate([picked.astype(BF16), *hi_lo(samples)], axis=0)


def merge(left, right, chosen):
    coords = jnp.concatenate([left[:FORM], right[:FORM]], axis=1)
    high = jnp.concatenate([left[FORM : FORM + SKEL], right[FORM : FORM + SKEL]], axis=0)
    low = jnp.concatenate([left[FORM + SKEL :], right[FORM + SKEL :]], axis=0)
    both = jnp.concatenate([high, low], axis=1)
    hot = one_hot(chosen, 2 * SKEL)
    picked = dot(coords, hot)
    kept = dot_tn(hot, both)
    weights = weigh(picked, coords)
    totals = jnp.sum(weights, axis=1, keepdims=True)
    w_hi, w_lo = hi_lo(weights)
    mixed = dot(w_hi, both)
    mixed = mixed[:, :LANES] + mixed[:, LANES:] + dot(w_lo, high)
    samples = kept[:, :LANES] + kept[:, LANES:] + mixed / totals
    return picked, samples


def rounds_of(leaf_count):
    rounds = [("sub", 1, 4), ("leaf", 1, 2)]
    d = 2
    while d < leaf_count:
        rounds.append(("leaf", d, 4 if 4 * d <= leaf_count else 2))
        d *= rounds[-1][2]
    return rounds


def pair_sum(target, source, probe):
    left = jnp.concatenate([target, tail_rows(half_squares(target.astype(F32)), 0, 3)], axis=0)
    right = jnp.concatenate([source, tail_rows(half_squares(source.astype(F32)), 3, 0)], axis=0)
    return dot(jnp.exp2(dot_tn(left, right) * SCALE).astype(BF16), probe)


def classify(block, shard_first, y):
    at = block - shard_first
    inside = (at >= 0) & (at < 4 * BLK)
    j = at & (BLK - 1)
    off = (lax.shift_right_arithmetic(at, 3) - y) & 3
    early = inside & (((off == 3) & (j < HALF)) | ((off == 1) & (j >= HALF)))
    side = jnp.where(at < 0, 0, 1)
    last = (side == (y & 1)) & ((j < HALF) == (y >= 2))
    edge = jnp.logical_not(inside) & jnp.logical_not(last)
    return [(inside & (off == 0), j), (early, j), (inside & (off == 2), j), (edge, side * BLK + j)]


def gather_kernel(
    leaf_count,
    lists,
    counts,
    points_hbm,
    probes_hbm,
    order_hbm,
    sets_hbm,
    merge_hbm,
    win_t,
    win_q,
    acc,
    root_ref,
    points,
    order,
    sets,
    chosen_rows,
    own_h,
    nodes,
    tree,
    final,
    own_t,
    own_q,
    early_t,
    early_q,
    fwd_t,
    fwd_q,
    edge_t,
    edge_q,
    plan,
    in_sem,
    row_sem,
    keep_sem,
    own_send,
    own_recv,
    late_send,
    late_recv,
    fwd_send,
    fwd_recv,
    edge_send,
    edge_recv,
    tree_send,
    tree_recv,
):
    leaf = lax.axis_index("leaf")
    y = lax.axis_index("sub")
    rank = leaf * 4 + y
    first_block = rank * BLK
    y_minus = lax.rem(y + 3, 4)
    y_plus = lax.rem(y + 1, 4)
    y_far = lax.rem(y + 2, 4)
    mine = BLK + y * BLK
    plus = (leaf, y_plus)
    minus = (leaf, y_minus)
    up = (lax.rem(leaf + 1, leaf_count), y)
    down = (lax.rem(leaf + leaf_count - 1, leaf_count), y)
    rounds = rounds_of(leaf_count)

    def partner(axis, d, n, k):
        place = y if axis == "sub" else leaf
        me = lax.rem(place // d, n)
        there = place + (lax.rem(me + k, n) - me) * d
        return me, ((leaf, there) if axis == "sub" else (there, y))

    inputs = [
        pltpu.make_async_copy(order_hbm, order, in_sem.at[0]),
        pltpu.make_async_copy(points_hbm, points, in_sem.at[1]),
        pltpu.make_async_copy(sets_hbm, sets, in_sem.at[2]),
        pltpu.make_async_copy(probes_hbm, own_q, in_sem.at[3]),
    ]
    wanted = [first_block + i for i in range(7)]
    row_at = []
    for axis, d, n in rounds:
        span = BLK * d if axis == "sub" else BLK * 4 * d
        first = first_block // (n * span) * (n * span)
        row_at.append(len(wanted))
        wanted += [first + span - 1] if n == 2 else [first + span - 1, first + 3 * span - 1, first + 2 * span - 1]
    rows = [
        pltpu.make_async_copy(merge_hbm.at[pl.ds(w, 1)], chosen_rows.at[pl.ds(i, 1)], row_sem.at[i])
        for i, w in enumerate(wanted)
    ]
    for copy in inputs + rows:
        copy.start()

    greet = [up, down]
    for axis, d, n in rounds:
        if axis == "sub" or d > 1:
            greet += [partner(axis, d, n, k)[1] for k in range(1, n)]
    barrier = pltpu.get_barrier_semaphore()
    for who in greet:
        pl.semaphore_signal(barrier, inc=1, device_id=who, device_id_type=MESH)
    pl.semaphore_wait(barrier, len(greet))

    wins = (win_t, win_q)
    owns = (own_t, own_q)
    earlies = (early_t, early_q)
    fwds = (fwd_t, fwd_q)
    edges = (edge_t, edge_q)
    near_side = y & 1
    soon = (y // 2) * HALF

    def remote(src, dst, send, recv, who):
        return pltpu.make_async_remote_copy(
            src_ref=src, dst_ref=dst, send_sem=send, recv_sem=recv, device_id=who, device_id_type=MESH
        )

    def own(kind, at, size):
        return (probes_hbm if kind else own_t).at[pl.ds(at, size)]

    def early(kind, way):
        return remote(
            own(kind, way * HALF, HALF),
            earlies[kind].at[pl.ds(way * HALF, HALF)],
            own_send.at[kind, way],
            own_recv.at[kind, way],
            minus if way else plus,
        )

    def late(kind, way, j):
        at = (1 - way) * HALF + j
        return remote(
            own(kind, at, 1),
            wins[kind].at[pl.ds(mine + at, 1)],
            late_send.at[kind, way, j],
            late_recv.at[kind, way, j],
            minus if way else plus,
        )

    def forward(kind, way, j):
        at = way * HALF + j
        return remote(
            earlies[kind].at[pl.ds(at, 1)],
            fwds[kind].at[pl.ds(at, 1)],
            fwd_send.at[kind, way, j],
            fwd_recv.at[kind, way, j],
            minus if way else plus,
        )

    def edge_copy(kind, side, j, source):
        if source == "own":
            src = own(kind, j, 1)
        elif source == "early":
            src = earlies[kind].at[pl.ds(j, 1)]
        elif source == "far":
            src = fwds[kind].at[pl.ds(j, 1)]
        else:
            src = wins[kind].at[pl.ds(BLK + (3 * BLK if side == 0 else 0) + j, 1)]
        there = wins[kind].at[pl.ds((0 if side == 0 else 5 * BLK) + j, 1)]
        return remote(
            src,
            there if source == "late" else edges[kind].at[pl.ds(side * BLK + j, 1)],
            edge_send.at[kind, side, j],
            edge_recv.at[kind, side, j],
            up if side == 0 else down,
        )

    has = (leaf < leaf_count - 1, leaf > 0)

    def start_edges(kinds, blocks, prev_when, next_when, source):
        for side, cond in ((0, prev_when), (1, next_when)):

            @pl.when(cond & has[side])
            def _(side=side):
                def body(j, carry):
                    for kind in kinds:
                        edge_copy(kind, side, j, source).start()
                    return carry

                lax.fori_loop(*blocks, body, 0)

    for way in range(2):
        early(1, way).start()
    start_edges((1,), (0, BLK), y == 3, y == 0, "own")

    inputs[0].wait()
    inputs[1].wait()

    def permute(i, carry):
        for k in range(2):
            b = 2 * i + k
            to = jnp.concatenate([order[pl.ds(b * 4 + q, 1), :] for q in range(4)], axis=1)
            at = pl.ds(pl.multiple_of(b * LEAF, LEAF), LEAF)
            coords = dot(points[:, at], one_hot(to, LEAF))
            own_t[b] = coords.astype(BF16)
            own_h[b] = tail_rows(half_squares(coords), 0, None)
        return carry

    lax.fori_loop(0, BLK // 2, permute, 0)
    for way in range(2):
        early(0, way).start()
    start_edges((0,), (0, BLK), y == 3, y == 0, "own")

    inputs[2].wait()
    inputs[3].wait()

    def leaf_nodes(i, carry):
        for k in range(4):
            b = 4 * i + k
            coords = jnp.concatenate([own_t[b], own_h[b]], axis=0)
            probe = own_q[b]
            hot = one_hot(sets[pl.ds(b, 1), :], LEAF)
            picked = dot(coords, hot)
            kept = dot_tn(hot, probe)
            weights = weigh(picked, coords)
            totals = jnp.sum(weights, axis=1, keepdims=True)
            w_hi, w_lo = hi_lo(weights)
            samples = kept + (dot(w_hi, probe) + dot(w_lo, probe)) / totals
            nodes[b] = node_of(picked, samples)
        return carry

    lax.fori_loop(0, BLK // 4, leaf_nodes, 0)
    for copy in rows:
        copy.wait()

    def row(i):
        return chosen_rows[i : i + 1, :]

    def merge_all(count, first, step):
        out = [node_of(*merge(nodes[2 * k], nodes[2 * k + 1], row(first + step * k))) for k in range(count)]
        for k in range(count):
            nodes[k] = out[k]

    merge_all(4, 0, 2)
    merge_all(2, 1, 4)
    state = merge(nodes[0], nodes[1], row(3))

    stocks = ((own_t, own_q), (early_t, early_q), (fwd_t, fwd_q), (edge_t, edge_q))
    spare = (0, 0, 0, jnp.where(leaf > 0, 0, BLK) + soon)
    first_step = [sum(STEPS[:c]) for c in range(4)]

    def plan_block(g, carry):
        count = counts[g]
        picks = [[[spare[c], 0] for _ in range(STEPS[c])] for c in range(4)]
        seen = [0, 0, 0, 0]
        for s in range(1, lists.shape[1]):
            for c, (there, at) in enumerate(classify(lists[g, s], leaf * 4 * BLK, y)):
                there = there & (s < count)
                for pick, i in zip(picks[c], range(STEPS[c])):
                    hit = there & (seen[c] == i)
                    pick[:] = jnp.where(hit, at, pick[0]), jnp.where(hit, 1, pick[1])
                seen[c] = seen[c] + there.astype(jnp.int32)
        for c in range(4):
            for i in range(STEPS[c]):
                plan[g, 2 * (first_step[c] + i)] = picks[c][i][0]
                plan[g, 2 * (first_step[c] + i) + 1] = picks[c][i][1]
        return carry

    def self_pairs(i, carry):
        for k in range(4):
            g = 4 * i + k
            acc[g] = pair_sum(own_t[g], own_t[g], own_q[g])
        return carry

    def pairs_from(c):
        width = 4 // STEPS[c]

        def body(i, carry):
            for h in range(width):
                g = width * i + h
                total = acc[g]
                for k in range(first_step[c], first_step[c] + STEPS[c]):
                    at = plan[g, 2 * k]
                    on = jnp.where(plan[g, 2 * k + 1] == 1, 1.0, 0.0)
                    total = total + pair_sum(own_t[g], stocks[c][0][at], stocks[c][1][at]) * on
                acc[g] = total
            return carry

        return body

    def begin(i, state):
        axis, d, n = rounds[i]
        me, _ = partner(axis, d, n, 1)
        ref = tree.at[i, me]
        tree[i, me] = node_of(*state)
        copies = [
            remote(ref, ref, tree_send.at[i, k - 1], tree_recv.at[i, k - 1], partner(axis, d, n, k)[1])
            for k in range(1, n)
        ]
        for copy in copies:
            copy.start()
        return copies

    def finish(i, copies):
        for copy in copies:
            copy.wait()
        at = row_at[i]
        if rounds[i][2] == 2:
            return merge(tree[i, 0], tree[i, 1], row(at))
        low = node_of(*merge(tree[i, 0], tree[i, 1], row(at)))
        high = node_of(*merge(tree[i, 2], tree[i, 3], row(at + 1)))
        return merge(low, high, row(at + 2))

    from_minus = (y == 0, y == 1)
    from_plus = (y == 2, y == 3)

    copies = begin(0, state)
    for way in range(2):
        late(1, way, 0).start()
    lax.fori_loop(0, BLK, plan_block, 0)
    lax.fori_loop(0, 2, self_pairs, 0)
    lax.fori_loop(0, 4, pairs_from(0), 0)
    for kind in (1, 0):
        for way in range(2):
            early(kind, way).wait_recv()

    def send_on(j, carry):
        for way in range(2):
            for kind in (1, 0):
                forward(kind, way, j).start()
        return carry

    lax.fori_loop(0, HALF, send_on, 0)
    start_edges((1, 0), (0, HALF), *from_minus, "early")
    start_edges((1, 0), (HALF, BLK), *from_plus, "early")
    for j in range(HALF):
        for way in range(2):
            for kind in (1, 0):
                if not (kind == 1 and j == 0):
                    late(kind, way, j).start()
    keep = []
    for kind in range(2):
        for k, (ref, there) in enumerate(
            (
                (owns[kind], mine),
                (earlies[kind].at[pl.ds(0, HALF)], BLK + y_minus * BLK),
                (earlies[kind].at[pl.ds(HALF, HALF)], BLK + y_plus * BLK + HALF),
            )
        ):
            size = HALF if k else BLK
            keep.append(pltpu.make_async_copy(ref, wins[kind].at[pl.ds(there, size)], keep_sem.at[kind, k]))
    for copy in keep:
        copy.start()
    state = finish(0, copies)

    def far(j, carry):
        for way in range(2):
            for kind in (1, 0):
                forward(kind, way, j).wait_recv()
        for side, cond in ((0, y == 1), (1, y == 2)):

            @pl.when(cond & has[side])
            def _(side=side):
                for way in range(2):
                    for kind in (1, 0):
                        edge_copy(kind, side, way * HALF + j, "far").start()

        return carry

    last = len(rounds) - 1
    e_step, f_step = pairs_from(1), pairs_from(2)
    if last == 4:
        fill = {
            2: ((e_step, 0, 1), (far, 0, 1), (e_step, 1, 2), (far, 1, 2)),
            3: ((e_step, 2, 3), (far, 2, 3), (e_step, 3, 4), (far, 3, 4)),
            4: ((f_step, 0, 2),),
        }
    else:
        fill = {last: ((e_step, 0, 4), (far, 0, 4), (f_step, 0, 2))}
    for i in range(1, len(rounds)):
        copies = begin(i, state)
        for what, start, end in fill.get(i, ()):
            lax.fori_loop(start, end, what, 0)
        state = finish(i, copies)
    for kind in range(2):
        copy = pltpu.make_async_copy(fwds[kind], wins[kind].at[pl.ds(BLK + y_far * BLK, BLK)], keep_sem.at[kind, 3])
        copy.start()
        keep.append(copy)
    final[...] = state[1]
    line = final[pl.ds(rank // 2 if leaf_count == 64 else 0, 1), :]
    line = jnp.broadcast_to(line, (8, LANES))
    root_ref[...] = jnp.where(lax.rem(rank, 2) == 1, pltpu.roll(line, DIM, 1), line)

    def second(j, carry):
        for way in range(2):
            for kind in (1, 0):
                late(kind, way, j).wait_recv()
        start_edges((1, 0), (HALF + j, HALF + j + 1), *from_minus, "late")
        start_edges((1, 0), (j, j + 1), *from_plus, "late")
        return carry

    def await_edges(near_from, others):
        for side in range(2):

            @pl.when(has[1 - side])
            def _(side=side):
                def body(j, carry):
                    for kind in range(2):
                        edge_copy(kind, side, j, "late" if not others else "far").wait_recv()
                    return carry

                @pl.when(near_side == side)
                def _():
                    lax.fori_loop(near_from, near_from + HALF, body, 0)

                if others:

                    @pl.when(near_side != side)
                    def _():
                        lax.fori_loop(0, BLK, body, 0)

    lax.fori_loop(0, 1, second, 0)
    lax.fori_loop(2, 4, f_step, 0)
    lax.fori_loop(1, HALF, second, 0)
    await_edges(soon, True)
    for kind in range(2):
        for k, (at, size, there) in enumerate(
            (
                (near_side * BLK + soon, HALF, near_side * 5 * BLK + soon),
                ((1 - near_side) * BLK, BLK, (1 - near_side) * 5 * BLK),
            )
        ):
            copy = pltpu.make_async_copy(
                edges[kind].at[pl.ds(at, size)], wins[kind].at[pl.ds(there, size)], keep_sem.at[kind, 4 + k]
            )
            copy.start()
            keep.append(copy)
    lax.fori_loop(0, BLK * STEPS[3] // 4, pairs_from(3), 0)

    for kind in range(2):
        for way in range(2):
            early(kind, way).wait_send()

    def drain(j, carry):
        for kind in range(2):
            for way in range(2):
                forward(kind, way, j).wait_send()
                late(kind, way, j).wait_send()
        return carry

    lax.fori_loop(0, HALF, drain, 0)
    for side in range(2):

        @pl.when(has[side])
        def _(side=side):
            def body(j, carry):
                for kind in range(2):
                    edge_copy(kind, side, j, "late").wait_send()
                return carry

            lax.fori_loop(0, BLK, body, 0)

    await_edges(HALF - soon, False)
    for copy in keep:
        copy.wait()


def near_kernel(lists, counts, win_t, win_q, part_ref, root_ref, out_ref, root_out, flat_g, flat_c, ends, acc, outs, sem_o):
    leaf = lax.axis_index("leaf")
    y = lax.axis_index("sub")
    mine = BLK + y * BLK

    def flatten(g, total):
        def one(s, carry):
            total, *seen = carry
            block = lists[g, s]
            done = False
            for c, (there, _) in enumerate(classify(block, leaf * 4 * BLK, y)):
                done = done | (there & (seen[c] < STEPS[c]))
                seen[c] = seen[c] + there.astype(jnp.int32)
            flat_g[total] = g
            flat_c[total] = block - (leaf * 4 * BLK - BLK)
            return (total + jnp.where(done, 0, 1), *seen)

        total = lax.fori_loop(1, counts[g], one, (total, *([jnp.int32(0)] * 4)))[0]
        ends[g] = total
        return total

    total = lax.fori_loop(0, BLK, flatten, jnp.int32(0))
    for i in range(PAIRS - 1):
        flat_g[total + i] = BLK
        flat_c[total + i] = mine
    acc[:BLK] = part_ref[...]
    acc[BLK] = jnp.zeros((LEAF, LANES), F32)

    def step(i, carry):
        for k in range(PAIRS):
            g = flat_g[i * PAIRS + k]
            c = flat_c[i * PAIRS + k]
            acc[g] += pair_sum(win_t[mine + jnp.minimum(g, BLK - 1)], win_t[c], win_q[c])
        return carry

    def block(g, i):
        until = jnp.maximum(i, (ends[g] + PAIRS - 1) // PAIRS)
        lax.fori_loop(i, until, step, 0)
        outs[g] = acc[g] * (LEAF**-0.5)
        pltpu.make_async_copy(outs.at[g], out_ref.at[g], sem_o.at[g]).start()
        return until

    lax.fori_loop(0, BLK, block, jnp.int32(0))
    root_out[...] = root_ref[0:1, :DIM]
    for g in range(BLK):
        pltpu.make_async_copy(outs.at[g], out_ref.at[g], sem_o.at[g]).wait()


def in_hbm(x):
    return pltpu.with_memory_space_constraint(x, pltpu.HBM)


def on_device(points, probes, order, near_lists, near_counts, leaf_sets, merge_sets):
    leaf_count = lax.axis_size("leaf")
    vmem = pl.BlockSpec(memory_space=pltpu.VMEM)
    hbm = pl.BlockSpec(memory_space=pltpu.HBM)
    smem = pl.BlockSpec(memory_space=pltpu.SMEM)
    window = 6 * BLK
    rounds = rounds_of(leaf_count)
    row_count = 7 + sum(n - 1 for _, _, n in rounds)
    dma = pltpu.SemaphoreType.DMA
    win_t, win_q, part, root = pl.pallas_call(
        functools.partial(gather_kernel, leaf_count),
        out_shape=(
            jax.ShapeDtypeStruct((window, DIM, LEAF), BF16),
            jax.ShapeDtypeStruct((window, LEAF, LANES), BF16),
            jax.ShapeDtypeStruct((BLK, LEAF, LANES), F32),
            jax.ShapeDtypeStruct((8, LANES), F32),
        ),
        in_specs=[smem, smem] + [hbm] * 5,
        out_specs=(vmem,) * 4,
        scratch_shapes=[
            pltpu.VMEM((DIM, BLK * LEAF), BF16),
            pltpu.VMEM((BLK * LEAF // LANES, LANES), jnp.int32),
            pltpu.VMEM((BLK, SKEL), jnp.int32),
            pltpu.VMEM((row_count, SKEL), jnp.int32),
            pltpu.VMEM((BLK, FORM - DIM, LEAF), BF16),
            pltpu.VMEM((BLK, NODE, LANES), BF16),
            pltpu.VMEM((len(rounds), 4, NODE, LANES), BF16),
            pltpu.VMEM((SKEL, LANES), F32),
            pltpu.VMEM((BLK, DIM, LEAF), BF16),
            pltpu.VMEM((BLK, LEAF, LANES), BF16),
            pltpu.VMEM((BLK, DIM, LEAF), BF16),
            pltpu.VMEM((BLK, LEAF, LANES), BF16),
            pltpu.VMEM((BLK, DIM, LEAF), BF16),
            pltpu.VMEM((BLK, LEAF, LANES), BF16),
            pltpu.VMEM((2 * BLK, DIM, LEAF), BF16),
            pltpu.VMEM((2 * BLK, LEAF, LANES), BF16),
            pltpu.SMEM((BLK, 2 * sum(STEPS)), jnp.int32),
            dma((4,)),
            dma((row_count,)),
            dma((2, 6)),
            dma((2, 2)),
            dma((2, 2)),
            dma((2, 2, HALF)),
            dma((2, 2, HALF)),
            dma((2, 2, HALF)),
            dma((2, 2, HALF)),
            dma((2, 2, BLK)),
            dma((2, 2, BLK)),
            dma((len(rounds), 3)),
            dma((len(rounds), 3)),
        ],
        compiler_params=pltpu.CompilerParams(
            collective_id=0, has_side_effects=True, vmem_limit_bytes=32 * 2**20
        ),
        name="gather_and_tree",
    )(*map(in_hbm, (near_lists, near_counts, points.T, probes.reshape(BLK, LEAF, LANES), order.reshape(-1, LANES), leaf_sets, merge_sets)))
    near, root = pl.pallas_call(
        near_kernel,
        out_shape=(jax.ShapeDtypeStruct((BLK, LEAF, LANES), F32), jax.ShapeDtypeStruct((1, DIM), F32)),
        in_specs=[smem, smem, vmem, vmem, vmem, vmem],
        out_specs=(hbm, vmem),
        scratch_shapes=[
            pltpu.SMEM((128,), jnp.int32),
            pltpu.SMEM((128,), jnp.int32),
            pltpu.SMEM((BLK,), jnp.int32),
            pltpu.VMEM((BLK + 1, LEAF, LANES), F32),
            pltpu.VMEM((BLK, LEAF, LANES), F32),
            dma((BLK,)),
        ],
        compiler_params=pltpu.CompilerParams(vmem_limit_bytes=32 * 2**20),
        name="near_field",
    )(in_hbm(near_lists), in_hbm(near_counts), win_t, win_q, part, root)
    return near.reshape(BLK * LEAF, LANES), root.reshape(DIM)


def solution(mesh):
    both = P(("leaf", "sub"), None)
    in_specs = (both, both, P(("leaf", "sub")), both, P(("leaf", "sub")), both, P())
    out_specs = (both, P(("leaf", "sub")))
    return jax.shard_map(on_device, mesh=mesh, in_specs=in_specs, out_specs=out_specs, check_vma=False)
```

```python
import functools

import jax
import jax.numpy as jnp
import numpy as np
from jax import lax
from jax.experimental import pallas as pl
from jax.experimental.pallas import tpu as pltpu
from jax.sharding import PartitionSpec as P

MESH = pl.DeviceIdType.MESH
BF16 = jnp.bfloat16
F32 = jnp.float32
LANES = 128
LEAF = 512
DIM = 64
FORM = DIM + 16
BLK = 8
HALF = 4
SKEL = 128
NODE = FORM + 2 * SKEL
PAIRS = 4
STEPS = (1, 2, 1, 1)
LOG2E = 1.4426950408889634
SCALE = 2.0 * LOG2E / DIM


def dot(a, b):
    return jnp.dot(a, b, preferred_element_type=F32)


def dot_tn(a, b):
    return lax.dot_general(a, b, (((0,), (0,)), ((), ())), preferred_element_type=F32)


def half_squares(coords):
    h = -0.5 * jnp.sum(coords * coords, axis=0, keepdims=True)
    h1 = h.astype(BF16).astype(F32)
    h2 = (h - h1).astype(BF16).astype(F32)
    h3 = (h - h1 - h2).astype(BF16).astype(F32)
    return h1, h2, h3


def tail_rows(squares, first, ones):
    shape = (FORM - DIM, squares[0].shape[1])
    row = lax.broadcasted_iota(jnp.int32, shape, 0)
    tail = jnp.zeros(shape, F32)
    if ones is not None:
        tail = jnp.where((row >= ones) & (row < ones + 3), 1.0, tail)
    for i, part in enumerate(squares):
        tail = jnp.where(row == first + i, part, tail)
    return tail.astype(BF16)


def one_hot(row, height):
    shape = (height, row.shape[1])
    return jnp.where(lax.broadcasted_iota(jnp.int32, shape, 0) == row, 1.0, 0.0).astype(BF16)


def weigh(picked, coords):
    row = lax.broadcasted_iota(jnp.int32, picked.shape, 0)
    left = jnp.where((row >= DIM) & (row < DIM + 3), 1.0, picked).astype(BF16)
    return jnp.exp2(dot_tn(left, coords) * SCALE)


def hi_lo(x):
    hi = x.astype(BF16)
    return hi, (x - hi.astype(F32)).astype(BF16)


def node_of(picked, samples):
    return jnp.concatenate([picked.astype(BF16), *hi_lo(samples)], axis=0)


def merge(left, right, chosen):
    coords = jnp.concatenate([left[:FORM], right[:FORM]], axis=1)
    high = jnp.concatenate([left[FORM : FORM + SKEL], right[FORM : FORM + SKEL]], axis=0)
    low = jnp.concatenate([left[FORM + SKEL :], right[FORM + SKEL :]], axis=0)
    both = jnp.concatenate([high, low], axis=1)
    hot = one_hot(chosen, 2 * SKEL)
    picked = dot(coords, hot)
    kept = dot_tn(hot, both)
    weights = weigh(picked, coords)
    totals = jnp.sum(weights, axis=1, keepdims=True)
    w_hi, w_lo = hi_lo(weights)
    mixed = dot(w_hi, both)
    mixed = mixed[:, :LANES] + mixed[:, LANES:] + dot(w_lo, high)
    samples = kept[:, :LANES] + kept[:, LANES:] + mixed / totals
    return picked, samples


def rounds_of(leaf_count):
    rounds = [("sub", 1, 4), ("leaf", 1, 2)]
    d = 2
    while d < leaf_count:
        rounds.append(("leaf", d, 4 if 4 * d <= leaf_count else 2))
        d *= rounds[-1][2]
    return rounds


def pair_sum(target, source, probe):
    left = jnp.concatenate([target, tail_rows(half_squares(target.astype(F32)), 0, 3)], axis=0)
    right = jnp.concatenate([source, tail_rows(half_squares(source.astype(F32)), 3, 0)], axis=0)
    return dot(jnp.exp2(dot_tn(left, right) * SCALE).astype(BF16), probe)


def classify(block, shard_first, y):
    at = block - shard_first
    inside = (at >= 0) & (at < 4 * BLK)
    j = at & (BLK - 1)
    off = (lax.shift_right_arithmetic(at, 3) - y) & 3
    early = inside & (((off == 3) & (j < HALF)) | ((off == 1) & (j >= HALF)))
    side = jnp.where(at < 0, 0, 1)
    last = (side == (y & 1)) & ((j < HALF) == (y >= 2))
    edge = jnp.logical_not(inside) & jnp.logical_not(last)
    return [(inside & (off == 0), j), (early, j), (inside & (off == 2), j), (edge, side * BLK + j)]


def class_table():
    table = np.zeros((4, 6 * BLK), np.int32)
    for y in range(4):
        for at in range(6 * BLK):
            shard, j = at // BLK - 1, at % BLK
            kind = 4
            if 0 <= shard < 4:
                off = (shard - y) % 4
                if off == 0:
                    kind = 0
                elif off == 2:
                    kind = 2
                elif (off == 3) == (j < HALF):
                    kind = 1
            elif not ((shard == 4) == (y % 2 == 1) and (j < HALF) == (y >= 2)):
                kind = 3
            table[y, at] = 8 * kind + (STEPS[kind] if kind < 4 else 0)
    return table


def gather_kernel(
    leaf_count,
    lists,
    counts,
    points_hbm,
    probes_hbm,
    order_hbm,
    sets_hbm,
    merge_hbm,
    win_t,
    win_q,
    acc,
    root_ref,
    points,
    order,
    sets,
    chosen_rows,
    own_h,
    nodes,
    tree,
    final,
    own_t,
    own_q,
    early_t,
    early_q,
    fwd_t,
    fwd_q,
    edge_t,
    edge_q,
    plan,
    in_sem,
    row_sem,
    keep_sem,
    own_send,
    own_recv,
    late_send,
    late_recv,
    fwd_send,
    fwd_recv,
    edge_send,
    edge_recv,
    tree_send,
    tree_recv,
):
    leaf = lax.axis_index("leaf")
    y = lax.axis_index("sub")
    rank = leaf * 4 + y
    first_block = rank * BLK
    y_minus = lax.rem(y + 3, 4)
    y_plus = lax.rem(y + 1, 4)
    y_far = lax.rem(y + 2, 4)
    mine = BLK + y * BLK
    plus = (leaf, y_plus)
    minus = (leaf, y_minus)
    up = (lax.rem(leaf + 1, leaf_count), y)
    down = (lax.rem(leaf + leaf_count - 1, leaf_count), y)
    rounds = rounds_of(leaf_count)

    def partner(axis, d, n, k):
        place = y if axis == "sub" else leaf
        me = lax.rem(place // d, n)
        there = place + (lax.rem(me + k, n) - me) * d
        return me, ((leaf, there) if axis == "sub" else (there, y))

    inputs = [
        pltpu.make_async_copy(order_hbm, order, in_sem.at[0]),
        pltpu.make_async_copy(points_hbm, points, in_sem.at[1]),
        pltpu.make_async_copy(sets_hbm, sets, in_sem.at[2]),
        pltpu.make_async_copy(probes_hbm, own_q, in_sem.at[3]),
    ]
    wanted = [first_block + i for i in range(7)]
    row_at = []
    for axis, d, n in rounds:
        span = BLK * d if axis == "sub" else BLK * 4 * d
        first = first_block // (n * span) * (n * span)
        row_at.append(len(wanted))
        wanted += [first + span - 1] if n == 2 else [first + span - 1, first + 3 * span - 1, first + 2 * span - 1]
    rows = [
        pltpu.make_async_copy(merge_hbm.at[pl.ds(w, 1)], chosen_rows.at[pl.ds(i, 1)], row_sem.at[i])
        for i, w in enumerate(wanted)
    ]
    for copy in inputs + rows:
        copy.start()

    greet = [up, down]
    for axis, d, n in rounds:
        if axis == "sub" or d > 1:
            greet += [partner(axis, d, n, k)[1] for k in range(1, n)]
    barrier = pltpu.get_barrier_semaphore()
    for who in greet:
        pl.semaphore_signal(barrier, inc=1, device_id=who, device_id_type=MESH)
    pl.semaphore_wait(barrier, len(greet))

    wins = (win_t, win_q)
    owns = (own_t, own_q)
    earlies = (early_t, early_q)
    fwds = (fwd_t, fwd_q)
    edges = (edge_t, edge_q)
    near_side = y & 1
    soon = (y // 2) * HALF

    def remote(src, dst, send, recv, who):
        return pltpu.make_async_remote_copy(
            src_ref=src, dst_ref=dst, send_sem=send, recv_sem=recv, device_id=who, device_id_type=MESH
        )

    def own(kind, at, size):
        return (probes_hbm if kind else own_t).at[pl.ds(at, size)]

    def early(kind, way):
        return remote(
            own(kind, way * HALF, HALF),
            earlies[kind].at[pl.ds(way * HALF, HALF)],
            own_send.at[kind, way],
            own_recv.at[kind, way],
            minus if way else plus,
        )

    def late(kind, way, j):
        at = (1 - way) * HALF + j
        return remote(
            own(kind, at, 1),
            wins[kind].at[pl.ds(mine + at, 1)],
            late_send.at[kind, way, j],
            late_recv.at[kind, way, j],
            minus if way else plus,
        )

    def forward(kind, way, j):
        at = way * HALF + j
        return remote(
            earlies[kind].at[pl.ds(at, 1)],
            fwds[kind].at[pl.ds(at, 1)],
            fwd_send.at[kind, way, j],
            fwd_recv.at[kind, way, j],
            minus if way else plus,
        )

    def edge_copy(kind, side, j, source):
        if source == "own":
            src = own(kind, j, 1)
        elif source == "early":
            src = earlies[kind].at[pl.ds(j, 1)]
        elif source == "far":
            src = fwds[kind].at[pl.ds(j, 1)]
        else:
            src = wins[kind].at[pl.ds(BLK + (3 * BLK if side == 0 else 0) + j, 1)]
        there = wins[kind].at[pl.ds((0 if side == 0 else 5 * BLK) + j, 1)]
        return remote(
            src,
            there if source == "late" else edges[kind].at[pl.ds(side * BLK + j, 1)],
            edge_send.at[kind, side, j],
            edge_recv.at[kind, side, j],
            up if side == 0 else down,
        )

    has = (leaf < leaf_count - 1, leaf > 0)

    def start_edges(kinds, blocks, prev_when, next_when, source):
        for side, cond in ((0, prev_when), (1, next_when)):

            @pl.when(cond & has[side])
            def _(side=side):
                def body(j, carry):
                    for kind in kinds:
                        edge_copy(kind, side, j, source).start()
                    return carry

                lax.fori_loop(*blocks, body, 0)

    for way in range(2):
        early(1, way).start()
    start_edges((1,), (0, BLK), y == 3, y == 0, "own")

    inputs[0].wait()
    inputs[1].wait()

    def permute(i, carry):
        for k in range(2):
            b = 2 * i + k
            to = jnp.concatenate([order[pl.ds(b * 4 + q, 1), :] for q in range(4)], axis=1)
            at = pl.ds(pl.multiple_of(b * LEAF, LEAF), LEAF)
            coords = dot(points[:, at], one_hot(to, LEAF))
            own_t[b] = coords.astype(BF16)
            own_h[b] = tail_rows(half_squares(coords), 0, None)
        return carry

    lax.fori_loop(0, BLK // 2, permute, 0)
    for way in range(2):
        early(0, way).start()
    start_edges((0,), (0, BLK), y == 3, y == 0, "own")

    inputs[2].wait()
    inputs[3].wait()

    def leaf_nodes(i, carry):
        for k in range(4):
            b = 4 * i + k
            coords = jnp.concatenate([own_t[b], own_h[b]], axis=0)
            probe = own_q[b]
            hot = one_hot(sets[pl.ds(b, 1), :], LEAF)
            picked = dot(coords, hot)
            kept = dot_tn(hot, probe)
            weights = weigh(picked, coords)
            totals = jnp.sum(weights, axis=1, keepdims=True)
            w_hi, w_lo = hi_lo(weights)
            samples = kept + (dot(w_hi, probe) + dot(w_lo, probe)) / totals
            nodes[b] = node_of(picked, samples)
        return carry

    lax.fori_loop(0, BLK // 4, leaf_nodes, 0)
    for copy in rows:
        copy.wait()

    def row(i):
        return chosen_rows[i : i + 1, :]

    def merge_all(count, first, step):
        out = [node_of(*merge(nodes[2 * k], nodes[2 * k + 1], row(first + step * k))) for k in range(count)]
        for k in range(count):
            nodes[k] = out[k]

    merge_all(4, 0, 2)
    merge_all(2, 1, 4)
    state = merge(nodes[0], nodes[1], row(3))

    stocks = ((own_t, own_q), (early_t, early_q), (fwd_t, fwd_q), (edge_t, edge_q))
    spare = (0, 0, 0, jnp.where(leaf > 0, 0, BLK) + soon)
    first_step = [sum(STEPS[:c]) for c in range(4)]

    def plan_block(g, carry):
        count = counts[g]
        picks = [[[spare[c], 0] for _ in range(STEPS[c])] for c in range(4)]
        seen = [0, 0, 0, 0]
        for s in range(1, lists.shape[1]):
            for c, (there, at) in enumerate(classify(lists[g, s], leaf * 4 * BLK, y)):
                there = there & (s < count)
                for pick, i in zip(picks[c], range(STEPS[c])):
                    hit = there & (seen[c] == i)
                    pick[:] = jnp.where(hit, at, pick[0]), jnp.where(hit, 1, pick[1])
                seen[c] = seen[c] + there.astype(jnp.int32)
        for c in range(4):
            for i in range(STEPS[c]):
                plan[g, 2 * (first_step[c] + i)] = picks[c][i][0]
                plan[g, 2 * (first_step[c] + i) + 1] = picks[c][i][1]
        return carry

    def self_pairs(i, carry):
        for k in range(4):
            g = 4 * i + k
            acc[g] = pair_sum(own_t[g], own_t[g], own_q[g])
        return carry

    def pairs_from(c):
        width = 4 // STEPS[c]

        def body(i, carry):
            for h in range(width):
                g = width * i + h
                total = acc[g]
                for k in range(first_step[c], first_step[c] + STEPS[c]):
                    at = plan[g, 2 * k]
                    on = jnp.where(plan[g, 2 * k + 1] == 1, 1.0, 0.0)
                    total = total + pair_sum(own_t[g], stocks[c][0][at], stocks[c][1][at]) * on
                acc[g] = total
            return carry

        return body

    def begin(i, state):
        axis, d, n = rounds[i]
        me, _ = partner(axis, d, n, 1)
        ref = tree.at[i, me]
        tree[i, me] = node_of(*state)
        copies = [
            remote(ref, ref, tree_send.at[i, k - 1], tree_recv.at[i, k - 1], partner(axis, d, n, k)[1])
            for k in range(1, n)
        ]
        for copy in copies:
            copy.start()
        return copies

    def finish(i, copies):
        for copy in copies:
            copy.wait()
        at = row_at[i]
        if rounds[i][2] == 2:
            return merge(tree[i, 0], tree[i, 1], row(at))
        low = node_of(*merge(tree[i, 0], tree[i, 1], row(at)))
        high = node_of(*merge(tree[i, 2], tree[i, 3], row(at + 1)))
        return merge(low, high, row(at + 2))

    from_minus = (y == 0, y == 1)
    from_plus = (y == 2, y == 3)

    own_step = pairs_from(0)
    copies = begin(0, state)
    for way in range(2):
        late(1, way, 0).start()
    lax.fori_loop(0, BLK, plan_block, 0)
    lax.fori_loop(0, 2, self_pairs, 0)
    lax.fori_loop(0, 2, own_step, 0)
    for kind in (1, 0):
        for way in range(2):
            early(kind, way).wait_recv()

    def send_on(j, carry):
        for way in range(2):
            for kind in (1, 0):
                forward(kind, way, j).start()
        return carry

    lax.fori_loop(0, HALF, send_on, 0)
    start_edges((1, 0), (0, HALF), *from_minus, "early")
    start_edges((1, 0), (HALF, BLK), *from_plus, "early")
    for j in range(HALF):
        for way in range(2):
            for kind in (1, 0):
                if not (kind == 1 and j == 0):
                    late(kind, way, j).start()
    keep = []
    for kind in range(2):
        for k, (ref, there) in enumerate(
            (
                (owns[kind], mine),
                (earlies[kind].at[pl.ds(0, HALF)], BLK + y_minus * BLK),
                (earlies[kind].at[pl.ds(HALF, HALF)], BLK + y_plus * BLK + HALF),
            )
        ):
            size = HALF if k else BLK
            keep.append(pltpu.make_async_copy(ref, wins[kind].at[pl.ds(there, size)], keep_sem.at[kind, k]))
    for copy in keep:
        copy.start()
    state = finish(0, copies)

    def far(j, carry):
        for way in range(2):
            for kind in (1, 0):
                forward(kind, way, j).wait_recv()
        for side, cond in ((0, y == 1), (1, y == 2)):

            @pl.when(cond & has[side])
            def _(side=side):
                for way in range(2):
                    for kind in (1, 0):
                        edge_copy(kind, side, way * HALF + j, "far").start()

        return carry

    last = len(rounds) - 1
    e_step, f_step = pairs_from(1), pairs_from(2)
    if last == 4:
        fill = {
            2: ((e_step, 0, 1), (far, 0, 1), (e_step, 1, 2), (far, 1, 2)),
            3: ((e_step, 2, 3), (far, 2, 3), (e_step, 3, 4), (far, 3, 4)),
            4: ((f_step, 0, 2),),
        }
    else:
        fill = {last: ((e_step, 0, 4), (far, 0, 4), (f_step, 0, 2))}
    for i in range(1, len(rounds)):
        copies = begin(i, state)
        for what, start, end in fill.get(i, ()):
            lax.fori_loop(start, end, what, 0)
        state = finish(i, copies)
    for kind in range(2):
        copy = pltpu.make_async_copy(fwds[kind], wins[kind].at[pl.ds(BLK + y_far * BLK, BLK)], keep_sem.at[kind, 3])
        copy.start()
        keep.append(copy)
    final[...] = state[1]
    line = final[pl.ds(rank // 2 if leaf_count == 64 else 0, 1), :]
    line = jnp.broadcast_to(line, (8, LANES))
    root_ref[...] = jnp.where(lax.rem(rank, 2) == 1, pltpu.roll(line, DIM, 1), line)

    def second(j, carry):
        for way in range(2):
            for kind in (1, 0):
                late(kind, way, j).wait_recv()
        start_edges((1, 0), (HALF + j, HALF + j + 1), *from_minus, "late")
        start_edges((1, 0), (j, j + 1), *from_plus, "late")
        return carry

    def await_edges(near_from, others):
        for side in range(2):

            @pl.when(has[1 - side])
            def _(side=side):
                def body(j, carry):
                    for kind in range(2):
                        edge_copy(kind, side, j, "late" if not others else "far").wait_recv()
                    return carry

                @pl.when(near_side == side)
                def _():
                    lax.fori_loop(near_from, near_from + HALF, body, 0)

                if others:

                    @pl.when(near_side != side)
                    def _():
                        lax.fori_loop(0, BLK, body, 0)

    lax.fori_loop(0, 1, second, 0)
    for kind in range(2):
        for way in range(2):
            early(kind, way).wait_send()

    def drain_forwards(j, carry):
        for kind in range(2):
            for way in range(2):
                forward(kind, way, j).wait_send()
        return carry

    lax.fori_loop(0, HALF, drain_forwards, 0)
    lax.fori_loop(1, HALF, second, 0)
    await_edges(soon, True)
    for kind in range(2):
        for k, (at, size, there) in enumerate(
            (
                (near_side * BLK + soon, HALF, near_side * 5 * BLK + soon),
                ((1 - near_side) * BLK, BLK, (1 - near_side) * 5 * BLK),
            )
        ):
            copy = pltpu.make_async_copy(
                edges[kind].at[pl.ds(at, size)], wins[kind].at[pl.ds(there, size)], keep_sem.at[kind, 4 + k]
            )
            copy.start()
            keep.append(copy)
    lax.fori_loop(0, BLK * STEPS[3] // 4, pairs_from(3), 0)

    def drain(j, carry):
        for kind in range(2):
            for way in range(2):
                late(kind, way, j).wait_send()
        return carry

    lax.fori_loop(0, HALF, drain, 0)
    for side in range(2):

        @pl.when(has[side])
        def _(side=side):
            def body(j, carry):
                for kind in range(2):
                    edge_copy(kind, side, j, "late").wait_send()
                return carry

            lax.fori_loop(0, BLK, body, 0)

    await_edges(HALF - soon, False)
    for copy in keep:
        copy.wait()


def near_kernel(lists, counts, table, win_t, win_q, part_ref, root_ref, out_ref, root_out, flat_g, flat_c, ends, seen, acc, outs, sem_o):
    leaf = lax.axis_index("leaf")
    y = lax.axis_index("sub")
    mine = BLK + y * BLK

    def flatten(g, total):
        for c in range(5):
            seen[c] = 0

        def one(s, total):
            at = lists[g, s] - (leaf * 4 * BLK - BLK)
            entry = table[y, at]
            kind = lax.shift_right_arithmetic(entry, 3)
            before = seen[kind]
            seen[kind] = before + 1
            flat_g[total] = g
            flat_c[total] = at
            return total + jnp.where(before < (entry & 7), 0, 1)

        total = lax.fori_loop(1, counts[g], one, total)
        ends[g] = total
        return total

    total = lax.fori_loop(0, BLK, flatten, jnp.int32(0))
    for i in range(PAIRS - 1):
        flat_g[total + i] = BLK
        flat_c[total + i] = mine
    acc[:BLK] = part_ref[...]
    acc[BLK] = jnp.zeros((LEAF, LANES), F32)

    def step(i, carry):
        for k in range(PAIRS):
            g = flat_g[i * PAIRS + k]
            c = flat_c[i * PAIRS + k]
            acc[g] += pair_sum(win_t[mine + jnp.minimum(g, BLK - 1)], win_t[c], win_q[c])
        return carry

    def block(g, i):
        until = jnp.maximum(i, (ends[g] + PAIRS - 1) // PAIRS)
        lax.fori_loop(i, until, step, 0)
        outs[g] = acc[g] * (LEAF**-0.5)
        pltpu.make_async_copy(outs.at[g], out_ref.at[g], sem_o.at[g]).start()
        return until

    lax.fori_loop(0, BLK, block, jnp.int32(0))
    root_out[...] = root_ref[0:1, :DIM]
    for g in range(BLK):
        pltpu.make_async_copy(outs.at[g], out_ref.at[g], sem_o.at[g]).wait()


def in_hbm(x):
    return pltpu.with_memory_space_constraint(x, pltpu.HBM)


def on_device(points, probes, order, near_lists, near_counts, leaf_sets, merge_sets):
    leaf_count = lax.axis_size("leaf")
    vmem = pl.BlockSpec(memory_space=pltpu.VMEM)
    hbm = pl.BlockSpec(memory_space=pltpu.HBM)
    smem = pl.BlockSpec(memory_space=pltpu.SMEM)
    window = 6 * BLK
    rounds = rounds_of(leaf_count)
    row_count = 7 + sum(n - 1 for _, _, n in rounds)
    dma = pltpu.SemaphoreType.DMA
    win_t, win_q, part, root = pl.pallas_call(
        functools.partial(gather_kernel, leaf_count),
        out_shape=(
            jax.ShapeDtypeStruct((window, DIM, LEAF), BF16),
            jax.ShapeDtypeStruct((window, LEAF, LANES), BF16),
            jax.ShapeDtypeStruct((BLK, LEAF, LANES), F32),
            jax.ShapeDtypeStruct((8, LANES), F32),
        ),
        in_specs=[smem, smem] + [hbm] * 5,
        out_specs=(vmem,) * 4,
        scratch_shapes=[
            pltpu.VMEM((DIM, BLK * LEAF), BF16),
            pltpu.VMEM((BLK * LEAF // LANES, LANES), jnp.int32),
            pltpu.VMEM((BLK, SKEL), jnp.int32),
            pltpu.VMEM((row_count, SKEL), jnp.int32),
            pltpu.VMEM((BLK, FORM - DIM, LEAF), BF16),
            pltpu.VMEM((BLK, NODE, LANES), BF16),
            pltpu.VMEM((len(rounds), 4, NODE, LANES), BF16),
            pltpu.VMEM((SKEL, LANES), F32),
            pltpu.VMEM((BLK, DIM, LEAF), BF16),
            pltpu.VMEM((BLK, LEAF, LANES), BF16),
            pltpu.VMEM((BLK, DIM, LEAF), BF16),
            pltpu.VMEM((BLK, LEAF, LANES), BF16),
            pltpu.VMEM((BLK, DIM, LEAF), BF16),
            pltpu.VMEM((BLK, LEAF, LANES), BF16),
            pltpu.VMEM((2 * BLK, DIM, LEAF), BF16),
            pltpu.VMEM((2 * BLK, LEAF, LANES), BF16),
            pltpu.SMEM((BLK, 2 * sum(STEPS)), jnp.int32),
            dma((4,)),
            dma((row_count,)),
            dma((2, 6)),
            dma((2, 2)),
            dma((2, 2)),
            dma((2, 2, HALF)),
            dma((2, 2, HALF)),
            dma((2, 2, HALF)),
            dma((2, 2, HALF)),
            dma((2, 2, BLK)),
            dma((2, 2, BLK)),
            dma((len(rounds), 3)),
            dma((len(rounds), 3)),
        ],
        compiler_params=pltpu.CompilerParams(
            collective_id=0, has_side_effects=True, vmem_limit_bytes=32 * 2**20
        ),
        name="gather_and_tree",
    )(*map(in_hbm, (near_lists, near_counts, points.T, probes.reshape(BLK, LEAF, LANES), order.reshape(-1, LANES), leaf_sets, merge_sets)))
    near, root = pl.pallas_call(
        near_kernel,
        out_shape=(jax.ShapeDtypeStruct((BLK, LEAF, LANES), F32), jax.ShapeDtypeStruct((1, DIM), F32)),
        in_specs=[smem] * 3 + [vmem] * 4,
        out_specs=(hbm, vmem),
        scratch_shapes=[
            pltpu.SMEM((128,), jnp.int32),
            pltpu.SMEM((128,), jnp.int32),
            pltpu.SMEM((BLK,), jnp.int32),
            pltpu.SMEM((BLK,), jnp.int32),
            pltpu.VMEM((BLK + 1, LEAF, LANES), F32),
            pltpu.VMEM((BLK, LEAF, LANES), F32),
            dma((BLK,)),
        ],
        compiler_params=pltpu.CompilerParams(vmem_limit_bytes=32 * 2**20),
        name="near_field",
    )(in_hbm(near_lists), in_hbm(near_counts), in_hbm(jnp.asarray(class_table())), win_t, win_q, part, root)
    return near.reshape(BLK * LEAF, LANES), root.reshape(DIM)


def solution(mesh):
    both = P(("leaf", "sub"), None)
    in_specs = (both, both, P(("leaf", "sub")), both, P(("leaf", "sub")), both, P())
    out_specs = (both, P(("leaf", "sub")))
    return jax.shard_map(on_device, mesh=mesh, in_specs=in_specs, out_specs=out_specs, check_vma=False)
```
